32 devices in a mesh: row: 4 (over y, x), bus: 8 (over z, core).
Axes of the slice: x: 2, y: 2, z: 4, core: 2. Of those that a mesh axis runs over, the one named last changes fastest.
Arguments:
- monitored: bfloat16 [512, 32768], P('row', 'bus'), may hold values from -6 to 6
- outaged: bfloat16 [256, 32768], P('row', 'bus'), may hold values from -6 to 6
- bus_weight: float32 [32768], P('bus'), may hold values from 0.5 to 4
- lodf_table: float32 [1024], replicated, may hold values from -1.5 to 1.5
- mon_id: int32 [2048], P('row'), may hold values from 0 to 511
- out_id: int32 [2048], P('row'), may hold values from 0 to 255
- lodf_idx: int32 [2048], P('row'), may hold values from 0 to 1023
Outputs:
- gram: float32 [2048, 2048], P('row', 'bus')
The draws below stay inside these ranges and needn't reach their ends.
All inputs are finite; a program needn't handle non-finite values.
Results may differ from the reference program's by a relative error of at most 0.0007.
Values may be sent and summed in bfloat16 or wider, within the bound.
A program may use at most 128 MiB of HBM per device.

```python
import math
import jax
import jax.numpy as jnp
import numpy as np

NB = 32768
NLODF = 1024
K = 2048
NMON = 512
NOUT = 256


def touch_ends(result, rng, smallest, largest):
    spot = [jax.random.randint(jax.random.fold_in(rng, axis), (), 0, length) for axis, length in enumerate(result.shape)]
    main_axis = result.shape.index(max(result.shape))
    next_to = spot[:main_axis] + [(spot[main_axis] + 1) % result.shape[main_axis]] + spot[main_axis + 1:]
    return result.at[tuple(spot)].set(smallest).at[tuple(next_to)].set(largest)


def level_of(stream_key, dims, pieces, least, high):
    def one(position, parts):
        steps = jax.random.uniform(jax.random.fold_in(jax.random.fold_in(stream_key, 6), position), (parts,), jnp.float32, least / len(pieces), high / len(pieces))
        return jnp.repeat(jnp.exp(steps), dims[position] // parts).reshape((-1,) + (1,) * (len(dims) - position - 1))

    gain = one(*pieces[0])
    for cut in pieces[1:]:
        gain = gain * one(*cut)
    return gain


def rank_table(number_of, lean):
    weights = [(1 << 20) // math.isqrt(rank ** lean) + 1 for rank in range(1, number_of + 1)]
    width = 1 + sum(weights) // (1 << 30)
    return np.cumsum(np.array([max(1, weight // width) for weight in weights]))


def skewed_ids(stream_key, dims, number_of, skew):
    listing = rank_table(number_of, skew)
    pick = jax.random.randint(jax.random.fold_in(stream_key, 1), dims, 0, int(listing[number_of - 1]))
    grade = jnp.searchsorted(jnp.asarray(listing, jnp.int32), pick, side="right")
    return jax.random.permutation(jax.random.fold_in(stream_key, 2), number_of)[grade].astype(jnp.int32)


def scatter_about(own_key, dims, scale, limit, split=(), dtype=jnp.bfloat16):
    result = scale * jax.random.normal(own_key, dims, jnp.float32)
    if split:
        result = result * level_of(own_key, dims, split, -0.22, 0.18)
    return jnp.clip(result, -limit, limit).astype(dtype)


def setup_inputs(seed: int = 0) -> dict:
    streams_of = jax.random.split(jax.random.key(seed), 8)
    monitored = scatter_about(streams_of[0], (NMON, NB), 1.0, 6.0, ((0, 4), (1, 8)))
    outaged = scatter_about(streams_of[1], (NOUT, NB), 1.0, 6.0, ((0, 4), (1, 8)))
    bus_weight = jnp.clip(jnp.exp(math.log(4.0) - 2.0794415 * jax.random.uniform(streams_of[2], (NB,), jnp.float32) ** level_of(streams_of[2], (NB,), ((0, 8),), -0.2, 0.2)), 0.5, 4.0)
    lodf_table = jnp.clip(jax.random.uniform(streams_of[3], (NLODF,), jnp.float32, -1.5, 1.5), -1.5, 1.5)
    mon_id = touch_ends(jax.random.randint(streams_of[4], (K,), 0, NMON), jax.random.fold_in(streams_of[4], 1), 0, NMON - 1).astype(jnp.int32)
    out_id = touch_ends(skewed_ids(streams_of[5], (K,), NOUT, 2), jax.random.fold_in(streams_of[5], 3), 0, NOUT - 1).astype(jnp.int32)
    lodf_idx = touch_ends(jax.random.randint(streams_of[6], (K,), 0, NLODF), jax.random.fold_in(streams_of[6], 1), 0, NLODF - 1).astype(jnp.int32)
    return dict(monitored=monitored, outaged=outaged, bus_weight=bus_weight, lodf_table=lodf_table, mon_id=mon_id, out_id=out_id, lodf_idx=lodf_idx)


def reference(monitored, outaged, bus_weight, lodf_table, mon_id, out_id, lodf_idx):
    coeff = jnp.take(lodf_table, lodf_idx, axis=0)
    base = jnp.take(monitored, mon_id, axis=0).astype(jnp.float32)
    extra = jnp.take(outaged, out_id, axis=0).astype(jnp.float32)
    post = (base + coeff[:, None] * extra).astype(jnp.bfloat16)
    weighted = (post.astype(jnp.float32) * (bus_weight / NB)[None, :]).astype(jnp.bfloat16)
    return jnp.dot(post, weighted.T, preferred_element_type=jnp.float32)
```

```python
import functools

import jax
import jax.numpy as jnp
from jax import lax
from jax.experimental import pallas as pl
from jax.experimental.pallas import tpu as pltpu
from jax.sharding import PartitionSpec as P

BLK = 128
BOUND = 6.0 * 6.0 * 4.0 * 1.01
F32 = jnp.float32
BF16 = jnp.bfloat16
I16 = jnp.int16
STAGED, DIRECT = 21, 14
MESH = pl.DeviceIdType.MESH


def split(v):
    a = v.astype(BF16)
    return a, (v - a.astype(F32)).astype(BF16)


def dot(a, b):
    return jnp.dot(a, b, preferred_element_type=F32)


def dot_t(a, b):
    return lax.dot_general(a, b, (((1,), (1,)), ((), ())), preferred_element_type=F32)


def encode(v, bound):
    u = jnp.abs(v) * (1.0 / bound)
    for _ in range(4):
        u = jnp.sqrt(u)
    u = jnp.minimum(u * 32767.0 + 0.5, 32767.0)
    return jnp.where(v < 0, -u, u).astype(jnp.int32).astype(jnp.int16)


def decode(q, bound):
    f = q.astype(jnp.int32).astype(F32) * (bound ** (1 / 16) / 32767.0)
    u = f
    for _ in range(4):
        u = u * u
    return jnp.where(f < 0, -u, u)


def down(lanes):
    n = lanes.shape[1]
    return jnp.broadcast_to(lanes, (128, n)).T


def factors(idx, table_t, entries):
    n = idx.shape[1]
    parts = []
    for lo in range(0, n, 128):
        total = jnp.zeros((1, 128), F32)
        for e in range(0, entries, 128):
            rows = lax.broadcasted_iota(jnp.int32, (128, 128), 0) + e
            hit = jnp.where(rows == idx[:, lo:lo + 128], table_t[e:e + 128, :], 0.0)
            total = total + jnp.sum(hit, axis=0, keepdims=True)
        parts.append(total)
    return jnp.concatenate(parts, axis=1)


class Stream:
    def __init__(self, refs, blocks, me, core, other, axes):
        (self.gp, self.cbuf, self.acc, self.e1, self.b1, self.s1, self.e2, self.b2, self.full,
         self.cs, self.cr, self.p1s, self.p1r, self.p2s, self.p2r,
         self.a1s, self.a1r, self.a2s, self.a2r, self.ds, self.dr) = refs
        self.blocks = blocks
        self.core, self.other = core, other
        (self.n1, self.i1, self.dev1), (self.n2, self.i2, self.dev2) = axes
        self.H = self.gp.shape[0] // 2
        self.h1 = self.H // self.n1
        self.pz = self.h1 // self.n2
        self.z_first = me
        self.at = 0

    def strip(self, k, x, xw):
        m = (k + 1) * BLK
        both = dot_t(x[:m, :], xw[k])
        self.gp[self.at:self.at + m, :] = both[:, :BLK] + both[:, BLK:]
        self.at += m

    def rows(self, start, count):
        return pl.ds(pl.multiple_of(start, 8), count)

    def send(self, src, dst, s, r, dev):
        c = pltpu.make_async_remote_copy(
            src_ref=src, dst_ref=dst, send_sem=s, recv_sem=r, device_id=dev, device_id_type=MESH)
        c.start()
        return c

    def pair_start(self):
        if self.gp.shape[0] > self.at:
            self.gp[self.at:, :] = jnp.zeros((self.gp.shape[0] - self.at, BLK), F32)
        self.c = [self.send(self.gp.at[self.rows((1 - self.core) * self.H, self.H), :], self.cbuf,
                            self.cs, self.cr, self.other)]

    def wait(self):
        for c in self.c:
            c.wait()

    def one_start(self):
        self.wait()
        total = self.gp[self.rows(self.core * self.H, self.H), :] + self.cbuf[...]
        self.acc[...] = total
        self.e1[...] = encode(total, BOUND).reshape(self.e1.shape)
        self.c = []
        for d in range(1, self.n1):
            q = lax.rem(self.i1 + d, self.n1)
            self.c.append(self.send(self.e1.at[q], self.b1.at[d - 1],
                                    self.p1s.at[d - 1], self.p1r.at[d - 1], self.dev1(q)))

    def two_start(self):
        self.wait()
        total = self.acc[self.rows(self.i1 * self.h1, self.h1), :]
        for d in range(1, self.n1):
            total = total + decode(self.b1[d - 1], BOUND)
        self.s1[...] = total
        self.e2[...] = encode(total, BOUND).reshape(self.e2.shape)
        self.c = []
        for d in range(1, self.n2):
            q = lax.rem(self.i2 + d, self.n2)
            self.c.append(self.send(self.e2.at[q], self.b2.at[d - 1],
                                    self.p2s.at[d - 1], self.p2r.at[d - 1], self.dev2(q)))

    def piece(self, z, r):
        i1, i2 = (z, r) if self.z_first else (r, z)
        return self.full.at[self.core, i1 * self.n2 + i2]

    def back_start(self):
        self.wait()
        total = self.s1[self.rows(self.i2 * self.pz, self.pz), :]
        for d in range(1, self.n2):
            total = total + decode(self.b2[d - 1], BOUND)
        if self.z_first:
            self.Z, self.zi, self.zdev = self.n1, self.i1, self.dev1
            self.R, self.r, self.rdev = self.n2, self.i2, self.dev2
        else:
            self.Z, self.zi, self.zdev = self.n2, self.i2, self.dev2
            self.R, self.r, self.rdev = self.n1, self.i1, self.dev1
        ref = self.piece(self.zi, self.r)
        ref[...] = encode(total, BOUND)
        self.zc = []
        for d in range(1, self.Z):
            self.zc.append(self.send(ref, ref, self.a1s.at[d - 1], self.a1r.at[d - 1],
                                     self.zdev(lax.rem(self.zi + d, self.Z))))
        self.c = []
        self.spread(0)

    def spread(self, e):
        ref = self.piece(lax.rem(self.zi + self.Z - e, self.Z), self.r)
        for d in range(1, self.R):
            self.c.append(self.send(ref, ref, self.a2s.at[e, d - 1], self.a2r.at[e, d - 1],
                                    self.rdev(lax.rem(self.r + d, self.R))))

    def spread_rest(self):
        for e in range(1, self.Z):
            self.zc[e - 1].wait()
            self.spread(e)

    def pair_back(self):
        self.wait()
        ref = self.full.at[self.core]
        self.c = [self.send(ref, ref, self.ds, self.dr, self.other)]


class Direct(Stream):
    def __init__(self, refs, blocks, core, other, axes):
        (self.gp, self.cbuf, self.acc, self.e1, self.b1, self.full,
         self.cs, self.cr, self.p1s, self.p1r, self.a1s, self.a1r, self.ds, self.dr) = refs
        self.blocks = blocks
        self.core, self.other = core, other
        self.Z, self.zi, self.R, self.r = axes
        self.H = self.gp.shape[0] // 2
        self.pz = self.H // (self.Z * self.R)
        self.at = 0

    def peers(self):
        for j in range(1, self.Z * self.R):
            z = lax.rem(self.zi + j // self.R, self.Z)
            r = lax.rem(self.r + j % self.R, self.R)
            yield j - 1, z * self.R + r, {"row": r, "bus": z * 2 + self.core}

    def one_start(self):
        self.wait()
        total = self.gp[self.rows(self.core * self.H, self.H), :] + self.cbuf[...]
        self.acc[...] = total
        self.e1[...] = encode(total, BOUND).reshape(self.e1.shape)
        self.c = [self.send(self.e1.at[at], self.b1.at[j], self.p1s.at[j], self.p1r.at[j], dev)
                  for j, at, dev in self.peers()]

    def back_start(self):
        self.wait()
        me = self.zi * self.R + self.r
        total = self.acc[self.rows(me * self.pz, self.pz), :]
        for j in range(self.Z * self.R - 1):
            total = total + decode(self.b1[j], BOUND)
        ref = self.full.at[self.core, me]
        ref[...] = encode(total, BOUND)
        self.c = [self.send(ref, ref, self.a1s.at[j], self.a1r.at[j], dev) for j, _, dev in self.peers()]


def select(ids, block, rows_each, dev_rows, axis, shape):
    p = lax.broadcasted_iota(jnp.int32, shape, axis)
    if axis == 1:
        p = p + block[1]
    shift = rows_each.bit_length() - 1
    line = lax.shift_right_logical(p, jnp.full(shape, shift, jnp.int32)) * (dev_rows - rows_each) + p
    return jnp.where(ids == line + block[0] * rows_each, 1.0, 0.0).astype(BF16)


def kernel(dims, mon_ref, out_ref, w_hbm, table_hbm, mid_hbm, oid_hbm, lid_hbm,
           gram_ref, w_ref, table_ref, mid_ref, oid_ref, lid_ref, small, x, xw, tt, ids, brow, t_o, t_m, x_s, x_r, i_s, i_r, own, own_i, *rest):
    R, B, nb_all = dims
    Z = B // 2
    r = lax.axis_index("row")
    b = lax.axis_index("bus")
    core = lax.rem(b, 2)
    zi = lax.div(b, 2)
    mrows, cols = mon_ref.shape
    orows = out_ref.shape[0]
    each = BLK // R
    cq = cols // R
    nblk_o, nblk_m = orows // each, mrows // each
    nblk = nblk_m + nblk_o
    kl = mid_ref.shape[1]
    kc = kl * R // B
    loads = []
    for i, (src, dst) in enumerate(((w_hbm, w_ref), (table_hbm, table_ref), (mid_hbm, mid_ref),
                                    (oid_hbm, oid_ref), (lid_hbm, lid_ref))):
        c = pltpu.make_async_copy(src, dst, small.at[i])
        c.start()
        loads.append(c)

    def row_dev(q):
        return {"row": q}

    def z_dev(q):
        return {"bus": q * 2 + core}

    pair_dev = {"bus": zi * 2 + (1 - core)}
    barrier = pltpu.get_barrier_semaphore()
    for d in range(1, R):
        pl.semaphore_signal(barrier, inc=1, device_id=row_dev(lax.rem(r + d, R)), device_id_type=MESH)
    for d in range(1, Z):
        pl.semaphore_signal(barrier, inc=1, device_id=z_dev(lax.rem(zi + d, Z)), device_id_type=MESH)
    pl.semaphore_signal(barrier, inc=1, device_id=pair_dev, device_id_type=MESH)
    pl.semaphore_wait(barrier, R - 1 + Z - 1 + 1)

    def source(k, q):
        ref, k = (out_ref, k) if k < nblk_o else (mon_ref, k - nblk_o)
        return ref.at[k * each:(k + 1) * each, pl.ds(pl.multiple_of(q * cq, 128), cq)]

    def target(k):
        return x.at[pl.ds(pl.multiple_of(k * BLK + r * each, each), each), :]

    id_copies = []
    for i, src in enumerate((mid_hbm, oid_hbm, lid_hbm)):
        for d in range(1, R):
            c = pltpu.make_async_remote_copy(
                src_ref=src, dst_ref=ids.at[i, r], send_sem=i_s.at[i, d - 1], recv_sem=i_r.at[i, d - 1],
                device_id=row_dev(lax.rem(r + d, R)), device_id_type=MESH)
            c.start()
            id_copies.append(c)
        c = pltpu.make_async_copy(src, ids.at[i, r], own_i.at[i])
        c.start()
        id_copies.append(c)

    chunks = []
    for k in range(nblk):
        chunk = []
        for d in range(1, R):
            q = lax.rem(r + d, R)
            c = pltpu.make_async_remote_copy(
                src_ref=source(k, q), dst_ref=target(k), send_sem=x_s.at[d - 1, k], recv_sem=x_r.at[d - 1, k],
                device_id=row_dev(q), device_id_type=MESH)
            c.start()
            chunk.append(c)
        c = pltpu.make_async_copy(source(k, r), target(k), own.at[k])
        c.start()
        chunk.append(c)
        chunks.append(chunk)
    for c in loads:
        c.wait()

    entries = table_ref.shape[1]
    for e in range(0, entries, 128):
        tt[e:e + 128, :] = down(table_ref[:, e:e + 128])
    c_row = down(factors(lid_ref[...], tt, entries))
    oid_t = down(oid_ref[...].astype(F32)).astype(jnp.int32)
    mid_t = down(mid_ref[...].astype(F32)).astype(jnp.int32)
    for k in range(nblk):
        for e in range(0, BLK, 128):
            at = slice(k * BLK + e, k * BLK + e + 128)
            if k < nblk_o:
                brow[:, at] = select(oid_t, (k, e), each, orows, 1, (kl, 128))
            else:
                brow[:, at] = select(mid_t, (k - nblk_o, e), each, mrows, 1, (kl, 128))
    scale = w_ref[:, pl.ds(pl.multiple_of(r * cq, 128), cq)] * (1.0 / nb_all)

    z_axis, row_axis = (Z, zi, z_dev), (R, r, row_dev)
    streams, at = [], 0
    for blocks, direct in plan(nblk):
        n = DIRECT if direct else STAGED
        refs = rest[at:at + n]
        at += n
        streams.append(Direct(refs, blocks, core, pair_dev, (Z, zi, R, r)) if direct else
                       Stream(refs, blocks, True, core, pair_dev, (z_axis, row_axis)))

    def arrive(k):
        for c in chunks[k]:
            c.wait()
        rows = slice(k * BLK, (k + 1) * BLK)
        v = x[rows, :].astype(F32) * scale
        h = v.astype(BF16)
        xw[k, :BLK, :] = h
        xw[k, BLK:, :] = (v - h.astype(F32)).astype(BF16)

    def begin(stream):
        for k in stream.blocks:
            arrive(k)
            stream.strip(k, x, xw)
        stream.pair_start()
        stream.one_start()

    s1, s2, s3, s4 = streams
    begin(s1)
    begin(s2)
    s1.two_start()
    begin(s3)
    s2.two_start()
    begin(s4)

    for c in id_copies:
        c.wait()
    owner = lax.div(b * kc, kl)
    begin = pl.multiple_of(lax.rem(b * kc, kl), 128)
    mid_c = ids[0, owner, :, pl.ds(begin, kc)]
    oid_c = ids[1, owner, :, pl.ds(begin, kc)]
    c_col = factors(ids[2, owner, :, pl.ds(begin, kc)], tt, entries)
    bcol = [select(oid_c, (k, 0), each, orows, 0, (BLK, kc)) for k in range(nblk_o)]
    bcol += [select(mid_c, (k, 0), each, mrows, 0, (BLK, kc)) for k in range(nblk_m)]

    t_o[...] = jnp.zeros_like(t_o)
    t_m[...] = jnp.zeros_like(t_m)
    cut = nblk_o * BLK

    def times(v, cols_of):
        total = None
        for p in split(v):
            total = dot(p, cols_of) if total is None else total + dot(p, cols_of)
        return total

    def gather(stream):
        stream.wait()
        at = 0
        both = decode(stream.full[...], BOUND).reshape(stream.gp.shape)
        for k in stream.blocks:
            m = (k + 1) * BLK
            strip = both[at:at + m, :]
            at += m
            t = t_o if k < nblk_o else t_m
            t[:m, :] = t[:m, :] + times(strip, bcol[k])
            rows = slice(k * BLK, m)
            above = min(k * BLK, cut)
            if above > 0:
                part = jnp.concatenate(bcol[:above // BLK], axis=0)
                t_o[rows, :] = t_o[rows, :] + times(strip[:above, :].T, part)
            if k * BLK > cut:
                part = jnp.concatenate(bcol[nblk_o:k], axis=0)
                t_m[rows, :] = t_m[rows, :] + times(strip[cut:k * BLK, :].T, part)

    s1.back_start()
    s2.back_start()
    s3.back_start()
    s4.back_start()
    s1.spread_rest()
    s2.spread_rest()
    s3.pair_back()
    s1.pair_back()
    s2.pair_back()
    gather(s3)
    s4.pair_back()
    gather(s1)
    gather(s2)
    gather(s4)
    t = t_m[...] + t_o[...] * c_col
    g_o = times_left(brow[:, :cut], t[:cut, :])
    g_m = times_left(brow[:, cut:], t[cut:, :])
    gram_ref[...] = g_m + g_o * jnp.concatenate([c_row] * (kc // 128), axis=1)


def times_left(s, v):
    a, b = split(v)
    return dot(s, a) + dot(s, b)


def plan(nblk):
    cuts = [0, nblk // 2, nblk - 2, nblk - 1, nblk]
    return [(range(a, b), i > 1) for i, (a, b) in enumerate(zip(cuts, cuts[1:]))]


def solution(mesh):
    R, B = mesh.shape["row"], mesh.shape["bus"]
    Z = B // 2

    def stream_scratch(blocks, n1, n2):
        unit = 8 * R * B
        packed = -(-(blocks * BLK) // unit) * unit
        H = packed // 2
        h1 = H // n1
        pz = h1 // n2
        dma = pltpu.SemaphoreType.DMA
        return [
            pltpu.VMEM((packed, BLK), F32),
            pltpu.VMEM((H, BLK), F32),
            pltpu.VMEM((H, BLK), F32),
            pltpu.VMEM((n1, h1, BLK), I16),
            pltpu.VMEM((n1 - 1, h1, BLK), I16),
            pltpu.VMEM((h1, BLK), F32),
            pltpu.VMEM((n2, pz, BLK), I16),
            pltpu.VMEM((n2 - 1, pz, BLK), I16),
            pltpu.VMEM((2, n1 * n2, pz, BLK), I16),
            dma, dma,
            dma((n1 - 1,)), dma((n1 - 1,)),
            dma((n2 - 1,)), dma((n2 - 1,)),
            dma((Z - 1,)), dma((Z - 1,)),
            dma((Z, R - 1)), dma((Z, R - 1)),
            dma, dma,
        ]

    def direct_scratch(blocks):
        unit = 8 * R * B
        packed = -(-(blocks * BLK) // unit) * unit
        H = packed // 2
        n = R * Z
        dma = pltpu.SemaphoreType.DMA
        return [
            pltpu.VMEM((packed, BLK), F32),
            pltpu.VMEM((H, BLK), F32),
            pltpu.VMEM((H, BLK), F32),
            pltpu.VMEM((n, H // n, BLK), I16),
            pltpu.VMEM((n - 1, H // n, BLK), I16),
            pltpu.VMEM((2, n, H // n, BLK), I16),
            dma, dma,
            dma((n - 1,)), dma((n - 1,)),
            dma((n - 1,)), dma((n - 1,)),
            dma, dma,
        ]

    def local(monitored, outaged, bus_weight, lodf_table, mon_id, out_id, lodf_idx):
        mrows, cols = monitored.shape
        orows = outaged.shape[0]
        n = (mrows + orows) * R
        cq = cols // R
        nblk = n // BLK
        kl = mon_id.shape[0]
        kc = kl * R // B
        vmem = pl.BlockSpec(memory_space=pltpu.VMEM)
        hbm = pl.BlockSpec(memory_space=pl.ANY)
        dma = pltpu.SemaphoreType.DMA
        streams = plan(nblk)
        return pl.pallas_call(
            functools.partial(kernel, (R, B, cols * B)),
            out_shape=jax.ShapeDtypeStruct((kl, kc), F32),
            in_specs=[hbm] * 7,
            out_specs=vmem,
            scratch_shapes=[
                pltpu.VMEM((1, cols), F32),
                pltpu.VMEM((1, lodf_table.shape[0]), F32),
                pltpu.VMEM((1, kl), jnp.int32),
                pltpu.VMEM((1, kl), jnp.int32),
                pltpu.VMEM((1, kl), jnp.int32),
                dma((5,)),
                pltpu.VMEM((n, cq), BF16),
                pltpu.VMEM((nblk, 2 * BLK, cq), BF16),
                pltpu.VMEM((lodf_table.shape[0], 128), F32),
                pltpu.VMEM((3, R, 1, kl), jnp.int32),
                pltpu.VMEM((kl, n), BF16),
                pltpu.VMEM((n, kc), F32),
                pltpu.VMEM((n, kc), F32),
                dma((R - 1, nblk)), dma((R - 1, nblk)),
                dma((3, R - 1)), dma((3, R - 1)),
                dma((nblk,)), dma((3,)),
            ] + [
                ref for blocks, direct in streams
                for ref in (direct_scratch(sum(k + 1 for k in blocks)) if direct else
                            stream_scratch(sum(k + 1 for k in blocks), Z, R))
            ],
            compiler_params=pltpu.CompilerParams(
                collective_id=0, has_side_effects=True, vmem_limit_bytes=60 * 1024 * 1024),
        )(monitored, outaged, bus_weight[None, :], lodf_table[None, :],
          mon_id[None, :], out_id[None, :], lodf_idx[None, :])

    in_specs = (P("row", "bus"), P("row", "bus"), P("bus"), P(), P("row"), P("row"), P("row"))
    return jax.shard_map(local, mesh=mesh, in_specs=in_specs, out_specs=P("row", "bus"), check_vma=False)
```

```python
import functools

import jax
import jax.numpy as jnp
from jax import lax
from jax.experimental import pallas as pl
from jax.experimental.pallas import tpu as pltpu
from jax.sharding import PartitionSpec as P

BLK = 128
BOUND = 6.0 * 6.0 * 4.0 * 1.01
F32 = jnp.float32
BF16 = jnp.bfloat16
I16 = jnp.int16
STAGED, DIRECT = 11, 8
MESH = pl.DeviceIdType.MESH


def split(v):
    a = v.astype(BF16)
    return a, (v - a.astype(F32)).astype(BF16)


def dot(a, b):
    return jnp.dot(a, b, preferred_element_type=F32)


def dot_t(a, b):
    return lax.dot_general(a, b, (((1,), (1,)), ((), ())), preferred_element_type=F32)


def encode(v, bound):
    u = jnp.abs(v) * (1.0 / bound)
    for _ in range(4):
        u = jnp.sqrt(u)
    u = jnp.minimum(u * 32767.0 + 0.5, 32767.0)
    return jnp.where(v < 0, -u, u).astype(jnp.int32).astype(jnp.int16)


def decode(q, bound):
    f = q.astype(jnp.int32).astype(F32) * (bound ** (1 / 16) / 32767.0)
    u = f
    for _ in range(4):
        u = u * u
    return jnp.where(f < 0, -u, u)


def down(lanes):
    n = lanes.shape[1]
    return jnp.broadcast_to(lanes, (128, n)).T


def factors(idx, table_t, entries):
    n = idx.shape[1]
    parts = []
    for lo in range(0, n, 128):
        total = jnp.zeros((1, 128), F32)
        for e in range(0, entries, 128):
            rows = lax.broadcasted_iota(jnp.int32, (128, 128), 0) + e
            hit = jnp.where(rows == idx[:, lo:lo + 128], table_t[e:e + 128, :], 0.0)
            total = total + jnp.sum(hit, axis=0, keepdims=True)
        parts.append(total)
    return jnp.concatenate(parts, axis=1)


def arrived(ref, sem):
    pltpu.make_async_copy(ref, ref, sem).wait()


def send(src, dst, s, r, dev):
    pltpu.make_async_remote_copy(
        src_ref=src, dst_ref=dst, send_sem=s, recv_sem=r, device_id=dev, device_id_type=MESH).start()


class Stream:
    def setup(self, blocks, core, other):
        self.blocks = blocks
        self.core, self.other = core, other
        self.H = self.gp.shape[0] // 2
        self.at = 0

    def strip(self, k, x, xw):
        m = (k + 1) * BLK
        both = dot_t(x[:m, :], xw[k])
        self.gp[self.at:self.at + m, :] = both[:, :BLK] + both[:, BLK:]
        self.at += m

    def rows(self, start, count):
        return pl.ds(pl.multiple_of(start, 8), count)

    def half(self, core):
        return self.gp.at[self.rows(core * self.H, self.H), :]

    def pair_start(self):
        if self.gp.shape[0] > self.at:
            self.gp[self.at:, :] = jnp.zeros((self.gp.shape[0] - self.at, BLK), F32)
        send(self.half(1 - self.core), self.cbuf, self.cs, self.cr, self.other)

    def pair_sum(self):
        arrived(self.cbuf, self.cr)
        total = self.half(self.core)[...] + self.cbuf[...]
        self.acc[...] = total
        self.e1[...] = encode(total, BOUND).reshape(self.e1.shape)

    def pair_back(self):
        ref = self.full.at[self.core]
        send(ref, ref, self.ds, self.dr, self.other)

    def whole(self):
        arrived(self.full.at[1 - self.core], self.dr)
        return decode(self.full[...], BOUND).reshape(self.gp.shape)


class Staged(Stream):
    def __init__(self, refs, blocks, core, other, axes):
        (self.gp, self.cbuf, self.acc, self.e1, self.b1, self.s1, self.e2, self.b2, self.full, sem, self.zr) = refs
        (self.cs, self.cr, self.p1s, self.p1r, self.p2s, self.p2r,
         self.a1s, self.a2s, self.a2r, self.ds, self.dr) = [sem.at[i] for i in range(STAGED)]
        self.setup(blocks, core, other)
        (self.Z, self.zi, self.zdev), (self.R, self.r, self.rdev) = axes
        self.h1 = self.H // self.Z
        self.pz = self.h1 // self.R

    def one_start(self):
        self.pair_sum()
        for d in range(1, self.Z):
            q = lax.rem(self.zi + d, self.Z)
            send(self.e1.at[q], self.b1.at[d - 1], self.p1s, self.p1r, self.zdev(q))

    def two_start(self):
        arrived(self.b1, self.p1r)
        total = self.acc[self.rows(self.zi * self.h1, self.h1), :]
        for d in range(1, self.Z):
            total = total + decode(self.b1[d - 1], BOUND)
        self.s1[...] = total
        self.e2[...] = encode(total, BOUND).reshape(self.e2.shape)
        for d in range(1, self.R):
            q = lax.rem(self.r + d, self.R)
            send(self.e2.at[q], self.b2.at[d - 1], self.p2s, self.p2r, self.rdev(q))

    def piece(self, z):
        return self.full.at[self.core, z * self.R + self.r]

    def back_start(self):
        arrived(self.b2, self.p2r)
        total = self.s1[self.rows(self.r * self.pz, self.pz), :]
        for d in range(1, self.R):
            total = total + decode(self.b2[d - 1], BOUND)
        ref = self.piece(self.zi)
        ref[...] = encode(total, BOUND)
        for d in range(1, self.Z):
            send(ref, ref, self.a1s, self.zr.at[d - 1], self.zdev(lax.rem(self.zi + d, self.Z)))
        self.spread(ref)

    def spread(self, ref):
        for d in range(1, self.R):
            send(ref, ref, self.a2s, self.a2r, self.rdev(lax.rem(self.r + d, self.R)))

    def spread_rest(self):
        for e in range(1, self.Z):
            ref = self.piece(lax.rem(self.zi + self.Z - e, self.Z))
            arrived(ref, self.zr.at[e - 1])
            self.spread(ref)

    def pair_back(self):
        arrived(self.full.at[self.core, :self.Z * (self.R - 1)], self.a2r)
        super().pair_back()

    def finish(self):
        arrived(self.cbuf, self.cs)
        arrived(self.b1, self.p1s)
        arrived(self.b2, self.p2s)
        arrived(self.full.at[0, :self.Z - 1], self.a1s)
        arrived(self.full.at[0, :self.Z * (self.R - 1)], self.a2s)
        arrived(self.full.at[0], self.ds)


class Direct(Stream):
    def __init__(self, refs, blocks, core, other, axes):
        self.gp, self.cbuf, self.acc, self.e1, self.b1, self.full, sem = refs
        (self.cs, self.cr, self.p1s, self.p1r, self.a1s, self.a1r, self.ds, self.dr) = [
            sem.at[i] for i in range(DIRECT)]
        self.setup(blocks, core, other)
        (self.Z, self.zi, _), (self.R, self.r, _) = axes
        self.N = self.Z * self.R
        self.pz = self.H // self.N

    def peers(self):
        for j in range(1, self.N):
            z = lax.rem(self.zi + j // self.R, self.Z)
            r = lax.rem(self.r + j % self.R, self.R)
            yield j - 1, z * self.R + r, {"row": r, "bus": z * 2 + self.core}

    def one_start(self):
        self.pair_sum()
        for j, at, dev in self.peers():
            send(self.e1.at[at], self.b1.at[j], self.p1s, self.p1r, dev)

    def back_start(self):
        arrived(self.b1, self.p1r)
        me = self.zi * self.R + self.r
        total = self.acc[self.rows(me * self.pz, self.pz), :]
        for j in range(self.N - 1):
            total = total + decode(self.b1[j], BOUND)
        ref = self.full.at[self.core, me]
        ref[...] = encode(total, BOUND)
        for _, _, dev in self.peers():
            send(ref, ref, self.a1s, self.a1r, dev)

    def pair_back(self):
        arrived(self.full.at[self.core, :self.N - 1], self.a1r)
        super().pair_back()

    def finish(self):
        arrived(self.cbuf, self.cs)
        arrived(self.b1, self.p1s)
        arrived(self.full.at[0, :self.N - 1], self.a1s)
        arrived(self.full.at[0], self.ds)


def select(ids, block, rows_each, dev_rows, axis, shape):
    p = lax.broadcasted_iota(jnp.int32, shape, axis)
    if axis == 1:
        p = p + block[1]
    shift = rows_each.bit_length() - 1
    line = lax.shift_right_logical(p, jnp.full(shape, shift, jnp.int32)) * (dev_rows - rows_each) + p
    return jnp.where(ids == line + block[0] * rows_each, 1.0, 0.0).astype(BF16)


def kernel(dims, mon_ref, out_ref, w_hbm, table_hbm, mid_hbm, oid_hbm, lid_hbm,
           gram_ref, w_ref, table_ref, mid_ref, oid_ref, lid_ref, small, x, xw, tt, ids, brow, t_o, t_m, x_s, x_r, i_s, i_r, *rest):
    R, B, nb_all = dims
    Z = B // 2
    r = lax.axis_index("row")
    b = lax.axis_index("bus")
    core = lax.rem(b, 2)
    zi = lax.div(b, 2)
    mrows, cols = mon_ref.shape
    orows = out_ref.shape[0]
    each = BLK // R
    cq = cols // R
    nblk_o, nblk_m = orows // each, mrows // each
    nblk = nblk_m + nblk_o
    n_sent = (R - 1) * (mrows + orows)
    kl = mid_ref.shape[1]
    kc = kl * R // B
    loads = []
    for i, (src, dst) in enumerate(((w_hbm, w_ref), (table_hbm, table_ref), (mid_hbm, mid_ref),
                                    (oid_hbm, oid_ref), (lid_hbm, lid_ref))):
        c = pltpu.make_async_copy(src, dst, small.at[i])
        c.start()
        loads.append(c)

    def row_dev(q):
        return {"row": q}

    def z_dev(q):
        return {"bus": q * 2 + core}

    pair_dev = {"bus": zi * 2 + (1 - core)}
    barrier = pltpu.get_barrier_semaphore()
    for d in range(1, R):
        pl.semaphore_signal(barrier, inc=1, device_id=row_dev(lax.rem(r + d, R)), device_id_type=MESH)
    for d in range(1, Z):
        pl.semaphore_signal(barrier, inc=1, device_id=z_dev(lax.rem(zi + d, Z)), device_id_type=MESH)
    pl.semaphore_signal(barrier, inc=1, device_id=pair_dev, device_id_type=MESH)
    pl.semaphore_wait(barrier, R - 1 + Z - 1 + 1)

    def source(k, q):
        ref, k = (out_ref, k) if k < nblk_o else (mon_ref, k - nblk_o)
        return ref.at[k * each:(k + 1) * each, pl.ds(pl.multiple_of(q * cq, 128), cq)]

    def target(k):
        return x.at[pl.ds(pl.multiple_of(k * BLK + r * each, each), each), :]

    for i, src in enumerate((mid_hbm, oid_hbm, lid_hbm)):
        for d in range(1, R):
            send(src, ids.at[i, r], i_s, i_r, row_dev(lax.rem(r + d, R)))
        pltpu.make_async_copy(src, ids.at[i, r], i_r).start()

    for k in range(nblk):
        for d in range(1, R):
            q = lax.rem(r + d, R)
            send(source(k, q), target(k), x_s, x_r.at[k], row_dev(q))
        pltpu.make_async_copy(source(k, r), target(k), x_r.at[k]).start()
    for c in loads:
        c.wait()

    entries = table_ref.shape[1]
    for e in range(0, entries, 128):
        tt[e:e + 128, :] = down(table_ref[:, e:e + 128])
    c_row = down(factors(lid_ref[...], tt, entries))
    oid_t = down(oid_ref[...].astype(F32)).astype(jnp.int32)
    mid_t = down(mid_ref[...].astype(F32)).astype(jnp.int32)
    for k in range(nblk):
        for e in range(0, BLK, 128):
            at = slice(k * BLK + e, k * BLK + e + 128)
            if k < nblk_o:
                brow[:, at] = select(oid_t, (k, e), each, orows, 1, (kl, 128))
            else:
                brow[:, at] = select(mid_t, (k - nblk_o, e), each, mrows, 1, (kl, 128))
    scale = w_ref[:, pl.ds(pl.multiple_of(r * cq, 128), cq)] * (1.0 / nb_all)

    z_axis, row_axis = (Z, zi, z_dev), (R, r, row_dev)
    streams, at = [], 0
    for blocks, direct in plan(nblk):
        kind, n = (Direct, 7) if direct else (Staged, 11)
        streams.append(kind(rest[at:at + n], blocks, core, pair_dev, (z_axis, row_axis)))
        at += n

    def arrive(k):
        rows = slice(k * BLK, (k + 1) * BLK)
        arrived(x.at[rows, :], x_r.at[k])
        v = x[rows, :].astype(F32) * scale
        h = v.astype(BF16)
        xw[k, :BLK, :] = h
        xw[k, BLK:, :] = (v - h.astype(F32)).astype(BF16)

    def begin(stream):
        for k in stream.blocks:
            arrive(k)
            stream.strip(k, x, xw)
        stream.pair_start()
        stream.one_start()

    s1, s2, s3, s4 = streams
    begin(s1)
    begin(s2)
    s1.two_start()
    begin(s3)
    s2.two_start()
    begin(s4)

    arrived(ids, i_r)
    owner = lax.div(b * kc, kl)
    begin = pl.multiple_of(lax.rem(b * kc, kl), 128)
    mid_c = ids[0, owner, :, pl.ds(begin, kc)]
    oid_c = ids[1, owner, :, pl.ds(begin, kc)]
    c_col = factors(ids[2, owner, :, pl.ds(begin, kc)], tt, entries)
    bcol = [select(oid_c, (k, 0), each, orows, 0, (BLK, kc)) for k in range(nblk_o)]
    bcol += [select(mid_c, (k, 0), each, mrows, 0, (BLK, kc)) for k in range(nblk_m)]

    t_o[...] = jnp.zeros_like(t_o)
    t_m[...] = jnp.zeros_like(t_m)
    cut = nblk_o * BLK

    def times(v, cols_of):
        total = None
        for p in split(v):
            total = dot(p, cols_of) if total is None else total + dot(p, cols_of)
        return total

    def gather(stream):
        at = 0
        both = stream.whole()
        for k in stream.blocks:
            m = (k + 1) * BLK
            strip = both[at:at + m, :]
            at += m
            t = t_o if k < nblk_o else t_m
            t[:m, :] = t[:m, :] + times(strip, bcol[k])
            rows = slice(k * BLK, m)
            above = min(k * BLK, cut)
            if above > 0:
                part = jnp.concatenate(bcol[:above // BLK], axis=0)
                t_o[rows, :] = t_o[rows, :] + times(strip[:above, :].T, part)
            if k * BLK > cut:
                part = jnp.concatenate(bcol[nblk_o:k], axis=0)
                t_m[rows, :] = t_m[rows, :] + times(strip[cut:k * BLK, :].T, part)

    s1.back_start()
    s2.back_start()
    s3.back_start()
    s4.back_start()
    s1.spread_rest()
    s2.spread_rest()
    s3.pair_back()
    s1.pair_back()
    s2.pair_back()
    gather(s3)
    s4.pair_back()
    gather(s1)
    gather(s2)
    gather(s4)
    t = t_m[...] + t_o[...] * c_col
    g_o = times_left(brow[:, :cut], t[:cut, :])
    g_m = times_left(brow[:, cut:], t[cut:, :])
    gram_ref[...] = g_m + g_o * jnp.concatenate([c_row] * (kc // 128), axis=1)
    arrived(x.at[:n_sent, :], x_s)
    arrived(ids.at[:, :R - 1], i_s)
    for stream in streams:
        stream.finish()


def times_left(s, v):
    a, b = split(v)
    return dot(s, a) + dot(s, b)


def plan(nblk):
    cuts = [0, nblk // 2, nblk - 2, nblk - 1, nblk]
    return [(range(a, b), i > 1) for i, (a, b) in enumerate(zip(cuts, cuts[1:]))]


def solution(mesh):
    R, B = mesh.shape["row"], mesh.shape["bus"]
    Z = B // 2

    def stream_scratch(blocks, n1, n2):
        unit = 8 * R * B
        packed = -(-(blocks * BLK) // unit) * unit
        H = packed // 2
        h1 = H // n1
        pz = h1 // n2
        dma = pltpu.SemaphoreType.DMA
        return [
            pltpu.VMEM((packed, BLK), F32),
            pltpu.VMEM((H, BLK), F32),
            pltpu.VMEM((H, BLK), F32),
            pltpu.VMEM((n1, h1, BLK), I16),
            pltpu.VMEM((n1 - 1, h1, BLK), I16),
            pltpu.VMEM((h1, BLK), F32),
            pltpu.VMEM((n2, pz, BLK), I16),
            pltpu.VMEM((n2 - 1, pz, BLK), I16),
            pltpu.VMEM((2, n1 * n2, pz, BLK), I16),
            dma((STAGED,)), dma((Z - 1,)),
        ]

    def direct_scratch(blocks):
        unit = 8 * R * B
        packed = -(-(blocks * BLK) // unit) * unit
        H = packed // 2
        n = R * Z
        dma = pltpu.SemaphoreType.DMA
        return [
            pltpu.VMEM((packed, BLK), F32),
            pltpu.VMEM((H, BLK), F32),
            pltpu.VMEM((H, BLK), F32),
            pltpu.VMEM((n, H // n, BLK), I16),
            pltpu.VMEM((n - 1, H // n, BLK), I16),
            pltpu.VMEM((2, n, H // n, BLK), I16),
            dma((DIRECT,)),
        ]

    def local(monitored, outaged, bus_weight, lodf_table, mon_id, out_id, lodf_idx):
        mrows, cols = monitored.shape
        orows = outaged.shape[0]
        n = (mrows + orows) * R
        cq = cols // R
        nblk = n // BLK
        kl = mon_id.shape[0]
        kc = kl * R // B
        vmem = pl.BlockSpec(memory_space=pltpu.VMEM)
        hbm = pl.BlockSpec(memory_space=pl.ANY)
        dma = pltpu.SemaphoreType.DMA
        streams = plan(nblk)
        return pl.pallas_call(
            functools.partial(kernel, (R, B, cols * B)),
            out_shape=jax.ShapeDtypeStruct((kl, kc), F32),
            in_specs=[hbm] * 7,
            out_specs=vmem,
            scratch_shapes=[
                pltpu.VMEM((1, cols), F32),
                pltpu.VMEM((1, lodf_table.shape[0]), F32),
                pltpu.VMEM((1, kl), jnp.int32),
                pltpu.VMEM((1, kl), jnp.int32),
                pltpu.VMEM((1, kl), jnp.int32),
                dma((5,)),
                pltpu.VMEM((n, cq), BF16),
                pltpu.VMEM((nblk, 2 * BLK, cq), BF16),
                pltpu.VMEM((lodf_table.shape[0], 128), F32),
                pltpu.VMEM((3, R, 1, kl), jnp.int32),
                pltpu.VMEM((kl, n), BF16),
                pltpu.VMEM((n, kc), F32),
                pltpu.VMEM((n, kc), F32),
                dma, dma((nblk,)), dma, dma,
            ] + [
                ref for blocks, direct in streams
                for ref in (direct_scratch(sum(k + 1 for k in blocks)) if direct else
                            stream_scratch(sum(k + 1 for k in blocks), Z, R))
            ],
            compiler_params=pltpu.CompilerParams(
                collective_id=0, has_side_effects=True, vmem_limit_bytes=60 * 1024 * 1024),
        )(monitored, outaged, bus_weight[None, :], lodf_table[None, :],
          mon_id[None, :], out_id[None, :], lodf_idx[None, :])

    in_specs = (P("row", "bus"), P("row", "bus"), P("bus"), P(), P("row"), P("row"), P("row"))
    return jax.shard_map(local, mesh=mesh, in_specs=in_specs, out_specs=P("row", "bus"), check_vma=False)
```

```python
import functools

import jax
import jax.numpy as jnp
from jax import lax
from jax.experimental import pallas as pl
from jax.experimental.pallas import tpu as pltpu
from jax.sharding import PartitionSpec as P

BLK = 128
BOUND = 6.0 * 6.0 * 4.0 * 1.01
F32 = jnp.float32
BF16 = jnp.bfloat16
I16 = jnp.int16
STAGED, DIRECT = 11, 8
MESH = pl.DeviceIdType.MESH


def split(v):
    a = v.astype(BF16)
    return a, (v - a.astype(F32)).astype(BF16)


def dot(a, b):
    return jnp.dot(a, b, preferred_element_type=F32)


def dot_t(a, b):
    return lax.dot_general(a, b, (((1,), (1,)), ((), ())), preferred_element_type=F32)


def encode(v, bound):
    u = jnp.abs(v) * (1.0 / bound)
    for _ in range(4):
        u = jnp.sqrt(u)
    u = jnp.minimum(u * 32767.0 + 0.5, 32767.0)
    return jnp.where(v < 0, -u, u).astype(jnp.int32).astype(jnp.int16)


def decode(q, bound):
    f = q.astype(jnp.int32).astype(F32) * (bound ** (1 / 16) / 32767.0)
    u = f
    for _ in range(4):
        u = u * u
    return jnp.where(f < 0, -u, u)


def down(lanes):
    n = lanes.shape[1]
    return jnp.broadcast_to(lanes, (128, n)).T


def factors(idx, table_t, entries):
    n = idx.shape[1]
    parts = []
    for lo in range(0, n, 128):
        total = jnp.zeros((1, 128), F32)
        for e in range(0, entries, 128):
            rows = lax.broadcasted_iota(jnp.int32, (128, 128), 0) + e
            hit = jnp.where(rows == idx[:, lo:lo + 128], table_t[e:e + 128, :], 0.0)
            total = total + jnp.sum(hit, axis=0, keepdims=True)
        parts.append(total)
    return jnp.concatenate(parts, axis=1)


def arrived(ref, sem):
    pltpu.make_async_copy(ref, ref, sem).wait()


def send(src, dst, s, r, dev):
    pltpu.make_async_remote_copy(
        src_ref=src, dst_ref=dst, send_sem=s, recv_sem=r, device_id=dev, device_id_type=MESH).start()


class Stream:
    def setup(self, blocks, core, other):
        self.blocks = blocks
        self.core, self.other = core, other
        self.H = self.gp.shape[0] // 2
        self.at = 0

    def strip(self, k, x, xw):
        m = (k + 1) * BLK
        both = dot_t(x[:m, :], xw[k])
        self.gp[self.at:self.at + m, :] = both[:, :BLK] + both[:, BLK:]
        self.at += m

    def strip_half(self, k, x, xw, core):
        rows = pl.ds(pl.multiple_of(core * self.H, BLK), self.H)
        both = dot_t(x[rows, :], xw[k])
        self.gp[rows, :] = both[:, :BLK] + both[:, BLK:]

    def rows(self, start, count):
        return pl.ds(pl.multiple_of(start, 8), count)

    def half(self, core):
        return self.gp.at[self.rows(core * self.H, self.H), :]

    def pair_start(self):
        if self.gp.shape[0] > self.at:
            self.gp[self.at:, :] = jnp.zeros((self.gp.shape[0] - self.at, BLK), F32)
        send(self.half(1 - self.core), self.cbuf, self.cs, self.cr, self.other)

    def pair_sum(self):
        arrived(self.cbuf, self.cr)
        total = self.half(self.core)[...] + self.cbuf[...]
        self.acc[...] = total
        self.e1[...] = encode(total, BOUND).reshape(self.e1.shape)

    def pair_back(self):
        ref = self.full.at[self.core]
        send(ref, ref, self.ds, self.dr, self.other)

    def whole(self):
        arrived(self.full.at[1 - self.core], self.dr)
        return decode(self.full[...], BOUND).reshape(self.gp.shape)


class Staged(Stream):
    def __init__(self, refs, blocks, core, other, axes):
        (self.gp, self.cbuf, self.acc, self.e1, self.b1, self.s1, self.e2, self.b2, self.full, sem, self.zr) = refs
        (self.cs, self.cr, self.p1s, self.p1r, self.p2s, self.p2r,
         self.a1s, self.a2s, self.a2r, self.ds, self.dr) = [sem.at[i] for i in range(STAGED)]
        self.setup(blocks, core, other)
        (self.Z, self.zi, self.zdev), (self.R, self.r, self.rdev) = axes
        self.h1 = self.H // self.Z
        self.pz = self.h1 // self.R

    def one_start(self):
        self.pair_sum()
        for d in range(1, self.Z):
            q = lax.rem(self.zi + d, self.Z)
            send(self.e1.at[q], self.b1.at[d - 1], self.p1s, self.p1r, self.zdev(q))

    def two_start(self):
        arrived(self.b1, self.p1r)
        total = self.acc[self.rows(self.zi * self.h1, self.h1), :]
        for d in range(1, self.Z):
            total = total + decode(self.b1[d - 1], BOUND)
        self.s1[...] = total
        self.e2[...] = encode(total, BOUND).reshape(self.e2.shape)
        for d in range(1, self.R):
            q = lax.rem(self.r + d, self.R)
            send(self.e2.at[q], self.b2.at[d - 1], self.p2s, self.p2r, self.rdev(q))

    def piece(self, z):
        return self.full.at[self.core, z * self.R + self.r]

    def back_start(self):
        arrived(self.b2, self.p2r)
        total = self.s1[self.rows(self.r * self.pz, self.pz), :]
        for d in range(1, self.R):
            total = total + decode(self.b2[d - 1], BOUND)
        ref = self.piece(self.zi)
        ref[...] = encode(total, BOUND)
        for d in range(1, self.Z):
            send(ref, ref, self.a1s, self.zr.at[d - 1], self.zdev(lax.rem(self.zi + d, self.Z)))
        self.spread(ref)

    def spread(self, ref):
        for d in range(1, self.R):
            send(ref, ref, self.a2s, self.a2r, self.rdev(lax.rem(self.r + d, self.R)))

    def spread_rest(self):
        for e in range(1, self.Z):
            ref = self.piece(lax.rem(self.zi + self.Z - e, self.Z))
            arrived(ref, self.zr.at[e - 1])
            self.spread(ref)

    def pair_back(self):
        arrived(self.full.at[self.core, :self.Z * (self.R - 1)], self.a2r)
        super().pair_back()

    def settle(self):
        arrived(self.cbuf, self.cs)
        arrived(self.b1, self.p1s)
        arrived(self.b2, self.p2s)

    def finish(self):
        arrived(self.full.at[0, :self.Z - 1], self.a1s)
        arrived(self.full.at[0, :self.Z * (self.R - 1)], self.a2s)
        arrived(self.full.at[0], self.ds)


class Direct(Stream):
    def __init__(self, refs, blocks, core, other, axes):
        self.gp, self.cbuf, self.acc, self.e1, self.b1, self.full, sem = refs
        (self.cs, self.cr, self.p1s, self.p1r, self.a1s, self.a1r, self.ds, self.dr) = [
            sem.at[i] for i in range(DIRECT)]
        self.setup(blocks, core, other)
        (self.Z, self.zi, _), (self.R, self.r, _) = axes
        self.N = self.Z * self.R
        self.pz = self.H // self.N

    def peers(self):
        for j in sorted(range(1, self.N), key=lambda j: (-min(j // self.R, self.Z - j // self.R), -(j % self.R))):
            z = lax.rem(self.zi + j // self.R, self.Z)
            r = lax.rem(self.r + j % self.R, self.R)
            yield j - 1, z * self.R + r, {"row": r, "bus": z * 2 + self.core}

    def one_start(self):
        self.pair_sum()
        for j, at, dev in self.peers():
            send(self.e1.at[at], self.b1.at[j], self.p1s, self.p1r, dev)

    def back_start(self):
        arrived(self.b1, self.p1r)
        me = self.zi * self.R + self.r
        total = self.acc[self.rows(me * self.pz, self.pz), :]
        for j in range(self.N - 1):
            total = total + decode(self.b1[j], BOUND)
        ref = self.full.at[self.core, me]
        ref[...] = encode(total, BOUND)
        for _, _, dev in self.peers():
            send(ref, ref, self.a1s, self.a1r, dev)

    def pair_back(self):
        arrived(self.full.at[self.core, :self.N - 1], self.a1r)
        super().pair_back()

    def settle(self):
        arrived(self.cbuf, self.cs)
        arrived(self.b1, self.p1s)

    def finish(self):
        arrived(self.full.at[0, :self.N - 1], self.a1s)
        arrived(self.full.at[0], self.ds)


def select(ids, block, rows_each, dev_rows, axis, shape):
    p = lax.broadcasted_iota(jnp.int32, shape, axis)
    if axis == 1:
        p = p + block[1]
    shift = rows_each.bit_length() - 1
    line = lax.shift_right_logical(p, jnp.full(shape, shift, jnp.int32)) * (dev_rows - rows_each) + p
    return jnp.where(ids == line + block[0] * rows_each, 1.0, 0.0).astype(BF16)


def kernel(dims, mon_ref, out_ref, w_hbm, table_hbm, mid_hbm, oid_hbm, lid_hbm,
           gram_ref, w_ref, table_ref, mid_ref, oid_ref, lid_ref, small, x, xw, tt, ids, brow, t_o, t_m, x_s, x_r, i_s, i_r, gram, g_s, *rest):
    R, B, nb_all = dims
    Z = B // 2
    r = lax.axis_index("row")
    b = lax.axis_index("bus")
    core = lax.rem(b, 2)
    zi = lax.div(b, 2)
    mrows, cols = mon_ref.shape
    orows = out_ref.shape[0]
    each = BLK // R
    cq = cols // R
    nblk_o, nblk_m = orows // each, mrows // each
    nblk = nblk_m + nblk_o
    n_sent = (R - 1) * (mrows + orows)
    kl = mid_ref.shape[1]
    kc = kl * R // B
    def row_dev(q):
        return {"row": q}

    def z_dev(q):
        return {"bus": q * 2 + core}

    pair_dev = {"bus": zi * 2 + (1 - core)}
    barrier = pltpu.get_barrier_semaphore()
    for d in range(1, R):
        pl.semaphore_signal(barrier, inc=1, device_id=row_dev(lax.rem(r + d, R)), device_id_type=MESH)
    for d in range(1, Z):
        pl.semaphore_signal(barrier, inc=1, device_id=z_dev(lax.rem(zi + d, Z)), device_id_type=MESH)
    pl.semaphore_signal(barrier, inc=1, device_id=pair_dev, device_id_type=MESH)
    loads = []
    for i, (src, dst) in enumerate(((w_hbm, w_ref), (table_hbm, table_ref), (mid_hbm, mid_ref),
                                    (oid_hbm, oid_ref), (lid_hbm, lid_ref))):
        c = pltpu.make_async_copy(src, dst, small.at[i])
        c.start()
        loads.append(c)
    pl.semaphore_wait(barrier, R - 1 + Z - 1 + 1)

    def source(k, q):
        ref, k = (out_ref, k) if k < nblk_o else (mon_ref, k - nblk_o)
        return ref.at[k * each:(k + 1) * each, pl.ds(pl.multiple_of(q * cq, 128), cq)]

    def target(k):
        return x.at[pl.ds(pl.multiple_of(k * BLK + r * each, each), each), :]

    def send_ids():
        for i, src in enumerate((mid_hbm, oid_hbm, lid_hbm)):
            for d in range(1, R):
                send(src, ids.at[i, r], i_s, i_r, row_dev(lax.rem(r + d, R)))
            pltpu.make_async_copy(src, ids.at[i, r], i_r).start()

    for k in range(nblk):
        for d in range(1, R):
            q = lax.rem(r + d, R)
            send(source(k, q), target(k), x_s, x_r.at[k], row_dev(q))
        pltpu.make_async_copy(source(k, r), target(k), x_r.at[k]).start()
        if k == 0:
            send_ids()
    for c in loads:
        c.wait()

    entries = table_ref.shape[1]
    for e in range(0, entries, 128):
        tt[e:e + 128, :] = down(table_ref[:, e:e + 128])
    c_row = down(factors(lid_ref[...], tt, entries))
    oid_t = down(oid_ref[...].astype(F32)).astype(jnp.int32)
    mid_t = down(mid_ref[...].astype(F32)).astype(jnp.int32)
    for k in range(nblk):
        for e in range(0, BLK, 128):
            at = slice(k * BLK + e, k * BLK + e + 128)
            if k < nblk_o:
                brow[:, at] = select(oid_t, (k, e), each, orows, 1, (kl, 128))
            else:
                brow[:, at] = select(mid_t, (k - nblk_o, e), each, mrows, 1, (kl, 128))
    scale = w_ref[:, pl.ds(pl.multiple_of(r * cq, 128), cq)] * (1.0 / nb_all)

    z_axis, row_axis = (Z, zi, z_dev), (R, r, row_dev)
    streams, at = [], 0
    for blocks, direct in plan(nblk):
        kind, n = (Direct, 7) if direct else (Staged, 11)
        streams.append(kind(rest[at:at + n], blocks, core, pair_dev, (z_axis, row_axis)))
        at += n

    def arrive(k):
        rows = slice(k * BLK, (k + 1) * BLK)
        arrived(x.at[rows, :], x_r.at[k])
        v = x[rows, :].astype(F32) * scale
        h = v.astype(BF16)
        xw[k, :BLK, :] = h
        xw[k, BLK:, :] = (v - h.astype(F32)).astype(BF16)

    def begin(stream):
        for k in stream.blocks:
            arrive(k)
            if len(stream.blocks) == 1 and (k + 1) * BLK == 2 * stream.H and stream.H % BLK == 0:
                stream.strip_half(k, x, xw, 1 - core)
                stream.at = 2 * stream.H
                stream.pair_start()
                stream.strip_half(k, x, xw, core)
                return
            stream.strip(k, x, xw)
        stream.pair_start()

    s1, s2, s3, s4 = streams
    begin(s1)
    s1.one_start()
    begin(s2)
    s2.one_start()
    s1.two_start()
    begin(s3)
    s3.one_start()
    begin(s4)
    s2.two_start()
    s4.one_start()

    arrived(ids, i_r)
    owner = lax.div(b * kc, kl)
    begin = pl.multiple_of(lax.rem(b * kc, kl), 128)
    mid_c = ids[0, owner, :, pl.ds(begin, kc)]
    oid_c = ids[1, owner, :, pl.ds(begin, kc)]
    c_col = factors(ids[2, owner, :, pl.ds(begin, kc)], tt, entries)
    bcol = [select(oid_c, (k, 0), each, orows, 0, (BLK, kc)) for k in range(nblk_o)]
    bcol += [select(mid_c, (k, 0), each, mrows, 0, (BLK, kc)) for k in range(nblk_m)]

    t_o[...] = jnp.zeros_like(t_o)
    t_m[...] = jnp.zeros_like(t_m)
    cut = nblk_o * BLK

    def times(v, cols_of):
        total = None
        for p in split(v):
            total = dot(p, cols_of) if total is None else total + dot(p, cols_of)
        return total

    def gather(stream):
        at = 0
        both = stream.whole()
        for k in stream.blocks:
            m = (k + 1) * BLK
            strip = both[at:at + m, :]
            at += m
            t = t_o if k < nblk_o else t_m
            t[:m, :] = t[:m, :] + times(strip, bcol[k])
            rows = slice(k * BLK, m)
            above = min(k * BLK, cut)
            if above > 0:
                part = jnp.concatenate(bcol[:above // BLK], axis=0)
                t_o[rows, :] = t_o[rows, :] + times(strip[:above, :].T, part)
            if k * BLK > cut:
                part = jnp.concatenate(bcol[nblk_o:k], axis=0)
                t_m[rows, :] = t_m[rows, :] + times(strip[cut:k * BLK, :].T, part)

    s1.back_start()
    s2.back_start()
    s3.back_start()
    s4.back_start()
    s1.spread_rest()
    s2.spread_rest()
    arrived(x.at[:n_sent, :], x_s)
    arrived(ids.at[:, :R - 1], i_s)
    for stream in streams:
        stream.settle()
    s3.pair_back()
    s1.pair_back()
    s2.pair_back()
    gather(s3)
    s4.pair_back()
    gather(s1)
    gather(s2)
    for stream in streams[:-1]:
        stream.finish()
    gather(s4)
    t = t_m[...] + t_o[...] * c_col
    t_hi, t_lo = split(t)
    step = kl // 4
    for at in range(0, kl, step):
        rows = slice(at, at + step)
        g_o = dot(brow[rows, :cut], t_hi[:cut, :]) + dot(brow[rows, :cut], t_lo[:cut, :])
        g_m = dot(brow[rows, cut:], t_hi[cut:, :]) + dot(brow[rows, cut:], t_lo[cut:, :])
        gram[rows, :] = g_m + g_o * jnp.concatenate([c_row[rows, :]] * (kc // 128), axis=1)
        pltpu.make_async_copy(gram.at[rows, :], gram_ref.at[rows, :], g_s).start()
    arrived(gram, g_s)
    s4.finish()


def plan(nblk):
    cuts = [0, nblk // 2, nblk - 2, nblk - 1, nblk]
    return [(range(a, b), i > 1) for i, (a, b) in enumerate(zip(cuts, cuts[1:]))]


def solution(mesh):
    R, B = mesh.shape["row"], mesh.shape["bus"]
    Z = B // 2

    def stream_scratch(blocks, n1, n2):
        unit = 8 * R * B
        packed = -(-(blocks * BLK) // unit) * unit
        H = packed // 2
        h1 = H // n1
        pz = h1 // n2
        dma = pltpu.SemaphoreType.DMA
        return [
            pltpu.VMEM((packed, BLK), F32),
            pltpu.VMEM((H, BLK), F32),
            pltpu.VMEM((H, BLK), F32),
            pltpu.VMEM((n1, h1, BLK), I16),
            pltpu.VMEM((n1 - 1, h1, BLK), I16),
            pltpu.VMEM((h1, BLK), F32),
            pltpu.VMEM((n2, pz, BLK), I16),
            pltpu.VMEM((n2 - 1, pz, BLK), I16),
            pltpu.VMEM((2, n1 * n2, pz, BLK), I16),
            dma((STAGED,)), dma((Z - 1,)),
        ]

    def direct_scratch(blocks):
        unit = 8 * R * B
        packed = -(-(blocks * BLK) // unit) * unit
        H = packed // 2
        n = R * Z
        dma = pltpu.SemaphoreType.DMA
        return [
            pltpu.VMEM((packed, BLK), F32),
            pltpu.VMEM((H, BLK), F32),
            pltpu.VMEM((H, BLK), F32),
            pltpu.VMEM((n, H // n, BLK), I16),
            pltpu.VMEM((n - 1, H // n, BLK), I16),
            pltpu.VMEM((2, n, H // n, BLK), I16),
            dma((DIRECT,)),
        ]

    def local(monitored, outaged, bus_weight, lodf_table, mon_id, out_id, lodf_idx):
        mrows, cols = monitored.shape
        orows = outaged.shape[0]
        n = (mrows + orows) * R
        cq = cols // R
        nblk = n // BLK
        kl = mon_id.shape[0]
        kc = kl * R // B
        hbm = pl.BlockSpec(memory_space=pl.ANY)
        dma = pltpu.SemaphoreType.DMA
        streams = plan(nblk)
        return pl.pallas_call(
            functools.partial(kernel, (R, B, cols * B)),
            out_shape=jax.ShapeDtypeStruct((kl, kc), F32),
            in_specs=[hbm] * 7,
            out_specs=hbm,
            scratch_shapes=[
                pltpu.VMEM((1, cols), F32),
                pltpu.VMEM((1, lodf_table.shape[0]), F32),
                pltpu.VMEM((1, kl), jnp.int32),
                pltpu.VMEM((1, kl), jnp.int32),
                pltpu.VMEM((1, kl), jnp.int32),
                dma((5,)),
                pltpu.VMEM((n, cq), BF16),
                pltpu.VMEM((nblk, 2 * BLK, cq), BF16),
                pltpu.VMEM((lodf_table.shape[0], 128), F32),
                pltpu.VMEM((3, R, 1, kl), jnp.int32),
                pltpu.VMEM((kl, n), BF16),
                pltpu.VMEM((n, kc), F32),
                pltpu.VMEM((n, kc), F32),
                dma, dma((nblk,)), dma, dma, pltpu.VMEM((kl, kc), F32), dma,
            ] + [
                ref for blocks, direct in streams
                for ref in (direct_scratch(sum(k + 1 for k in blocks)) if direct else
                            stream_scratch(sum(k + 1 for k in blocks), Z, R))
            ],
            compiler_params=pltpu.CompilerParams(
                collective_id=0, has_side_effects=True, vmem_limit_bytes=60 * 1024 * 1024),
        )(monitored, outaged, bus_weight[None, :], lodf_table[None, :],
          mon_id[None, :], out_id[None, :], lodf_idx[None, :])

    in_specs = (P("row", "bus"), P("row", "bus"), P("bus"), P(), P("row"), P("row"), P("row"))
    return jax.shard_map(local, mesh=mesh, in_specs=in_specs, out_specs=P("row", "bus"), check_vma=False)
```

```python
import functools
import math

import jax
import jax.numpy as jnp
from jax import lax
from jax.experimental import pallas as pl
from jax.experimental.pallas import tpu as pltpu
from jax.sharding import PartitionSpec as P

BLK = 128
TINY = 1e-30
BOUND = 6.0 * 6.0 * 4.0 * 1.01
F32 = jnp.float32
BF16 = jnp.bfloat16
I16 = jnp.int16
STAGED, DIRECT = 11, 8
MESH = pl.DeviceIdType.MESH


def split(v):
    a = v.astype(BF16)
    return a, (v - a.astype(F32)).astype(BF16)


def dot(a, b):
    return jnp.dot(a, b, preferred_element_type=F32)


def dot_t(a, b):
    return lax.dot_general(a, b, (((1,), (1,)), ((), ())), preferred_element_type=F32)


def encode(v, bound):
    u = jnp.log2(jnp.maximum(jnp.abs(v), TINY)) * (1 / 16) + math.log2(32767.0 / bound ** (1 / 16))
    u = jnp.minimum(jnp.exp2(u) + 0.5, 32767.0)
    return jnp.where(v < 0, -u, u).astype(jnp.int32).astype(I16)


def decode(q, bound):
    f = q.astype(jnp.int32).astype(F32) * (bound ** (1 / 16) / 32767.0)
    u = f
    for _ in range(4):
        u = u * u
    return jnp.where(f < 0, -u, u)


def down(lanes):
    n = lanes.shape[1]
    return jnp.broadcast_to(lanes, (128, n)).T


def factors(idx, table_t, entries):
    n = idx.shape[1]
    parts = []
    for lo in range(0, n, 128):
        total = jnp.zeros((1, 128), F32)
        for e in range(0, entries, 128):
            rows = lax.broadcasted_iota(jnp.int32, (128, 128), 0) + e
            hit = jnp.where(rows == idx[:, lo:lo + 128], table_t[e:e + 128, :], 0.0)
            total = total + jnp.sum(hit, axis=0, keepdims=True)
        parts.append(total)
    return jnp.concatenate(parts, axis=1)


def arrived(ref, sem):
    pltpu.make_async_copy(ref, ref, sem).wait()


def send(src, dst, s, r, dev):
    pltpu.make_async_remote_copy(
        src_ref=src, dst_ref=dst, send_sem=s, recv_sem=r, device_id=dev, device_id_type=MESH).start()


class Stream:
    def setup(self, blocks, core, other):
        self.blocks = blocks
        self.core, self.other = core, other
        self.H = self.gp.shape[0] // 2
        self.at = 0

    def strip(self, k, x, xw):
        m = (k + 1) * BLK
        both = dot_t(x[:m, :], xw[k])
        self.gp[self.at:self.at + m, :] = both[:, :BLK] + both[:, BLK:]
        self.at += m

    def strip_half(self, k, x, xw, core):
        rows = pl.ds(pl.multiple_of(core * self.H, BLK), self.H)
        both = dot_t(x[rows, :], xw[k])
        self.gp[rows, :] = both[:, :BLK] + both[:, BLK:]

    def rows(self, start, count):
        return pl.ds(pl.multiple_of(start, 8), count)

    def half(self, core):
        return self.gp.at[self.rows(core * self.H, self.H), :]

    def pair_start(self):
        if self.gp.shape[0] > self.at:
            self.gp[self.at:, :] = jnp.zeros((self.gp.shape[0] - self.at, BLK), F32)
        send(self.half(1 - self.core), self.cbuf, self.cs, self.cr, self.other)

    def pair_sum(self):
        arrived(self.cbuf, self.cr)
        total = self.half(self.core)[...] + self.cbuf[...]
        self.acc[...] = total
        self.e1[...] = encode(total, BOUND).reshape(self.e1.shape)

    def pair_back(self):
        ref = self.full.at[self.core]
        send(ref, ref, self.ds, self.dr, self.other)

    def whole(self):
        arrived(self.full.at[1 - self.core], self.dr)
        return decode(self.full[...], BOUND).reshape(self.gp.shape)


class Staged(Stream):
    def __init__(self, refs, blocks, core, other, axes):
        (self.gp, self.cbuf, self.acc, self.e1, self.b1, self.s1, self.e2, self.b2, self.full, sem, self.zr) = refs
        (self.cs, self.cr, self.p1s, self.p1r, self.p2s, self.p2r,
         self.a1s, self.a2s, self.a2r, self.ds, self.dr) = [sem.at[i] for i in range(STAGED)]
        self.setup(blocks, core, other)
        (self.Z, self.zi, self.zdev), (self.R, self.r, self.rdev) = axes
        self.h1 = self.H // self.Z
        self.pz = self.h1 // self.R

    def one_start(self):
        self.pair_sum()
        for d in range(1, self.Z):
            q = lax.rem(self.zi + d, self.Z)
            send(self.e1.at[q], self.b1.at[d - 1], self.p1s, self.p1r, self.zdev(q))

    def two_start(self):
        arrived(self.b1, self.p1r)
        total = self.acc[self.rows(self.zi * self.h1, self.h1), :]
        for d in range(1, self.Z):
            total = total + decode(self.b1[d - 1], BOUND)
        self.s1[...] = total
        self.e2[...] = encode(total, BOUND).reshape(self.e2.shape)
        for d in range(1, self.R):
            q = lax.rem(self.r + d, self.R)
            send(self.e2.at[q], self.b2.at[d - 1], self.p2s, self.p2r, self.rdev(q))

    def piece(self, z):
        return self.full.at[self.core, z * self.R + self.r]

    def back_start(self):
        arrived(self.b2, self.p2r)
        total = self.s1[self.rows(self.r * self.pz, self.pz), :]
        for d in range(1, self.R):
            total = total + decode(self.b2[d - 1], BOUND)
        ref = self.piece(self.zi)
        ref[...] = encode(total, BOUND)
        for d in range(1, self.Z):
            send(ref, ref, self.a1s, self.zr.at[d - 1], self.zdev(lax.rem(self.zi + d, self.Z)))
        self.spread(ref)

    def spread(self, ref):
        for d in range(1, self.R):
            send(ref, ref, self.a2s, self.a2r, self.rdev(lax.rem(self.r + d, self.R)))

    def spread_rest(self):
        for e in range(1, self.Z):
            ref = self.piece(lax.rem(self.zi + self.Z - e, self.Z))
            arrived(ref, self.zr.at[e - 1])
            self.spread(ref)

    def pair_back(self):
        arrived(self.full.at[self.core, :self.Z * (self.R - 1)], self.a2r)
        super().pair_back()

    def settle(self):
        arrived(self.cbuf, self.cs)
        arrived(self.b1, self.p1s)
        arrived(self.b2, self.p2s)

    def finish(self):
        arrived(self.full.at[0, :self.Z - 1], self.a1s)
        arrived(self.full.at[0, :self.Z * (self.R - 1)], self.a2s)
        arrived(self.full.at[0], self.ds)


class Direct(Stream):
    def __init__(self, refs, blocks, core, other, axes):
        self.gp, self.cbuf, self.acc, self.e1, self.b1, self.full, sem = refs
        (self.cs, self.cr, self.p1s, self.p1r, self.a1s, self.a1r, self.ds, self.dr) = [
            sem.at[i] for i in range(DIRECT)]
        self.setup(blocks, core, other)
        (self.Z, self.zi, _), (self.R, self.r, _) = axes
        self.N = self.Z * self.R
        self.pz = self.H // self.N

    def peers(self):
        for j in sorted(range(1, self.N), key=lambda j: (-min(j // self.R, self.Z - j // self.R), -(j % self.R))):
            z = lax.rem(self.zi + j // self.R, self.Z)
            r = lax.rem(self.r + j % self.R, self.R)
            yield j - 1, z * self.R + r, {"row": r, "bus": z * 2 + self.core}

    def one_start(self):
        self.pair_sum()
        for j, at, dev in self.peers():
            send(self.e1.at[at], self.b1.at[j], self.p1s, self.p1r, dev)

    def back_start(self):
        arrived(self.b1, self.p1r)
        me = self.zi * self.R + self.r
        total = self.acc[self.rows(me * self.pz, self.pz), :]
        for j in range(self.N - 1):
            total = total + decode(self.b1[j], BOUND)
        ref = self.full.at[self.core, me]
        ref[...] = encode(total, BOUND)
        for _, _, dev in self.peers():
            send(ref, ref, self.a1s, self.a1r, dev)

    def pair_back(self):
        arrived(self.full.at[self.core, :self.N - 1], self.a1r)
        super().pair_back()

    def settle(self):
        arrived(self.cbuf, self.cs)
        arrived(self.b1, self.p1s)

    def finish(self):
        arrived(self.full.at[0, :self.N - 1], self.a1s)
        arrived(self.full.at[0], self.ds)


def select(ids, block, rows_each, dev_rows, axis, shape):
    p = lax.broadcasted_iota(jnp.int32, shape, axis)
    if axis == 1:
        p = p + block[1]
    shift = rows_each.bit_length() - 1
    line = lax.shift_right_logical(p, jnp.full(shape, shift, jnp.int32)) * (dev_rows - rows_each) + p
    return jnp.where(ids == line + block[0] * rows_each, 1.0, 0.0).astype(BF16)


def kernel(dims, mon_ref, out_ref, w_hbm, table_hbm, mid_hbm, oid_hbm, lid_hbm,
           gram_ref, w_ref, table_ref, mid_ref, oid_ref, lid_ref, small, x, xw, tt, ids, brow, t_o, t_m, x_s, x_r, i_s, i_r, gram, g_s, *rest):
    R, B, nb_all = dims
    Z = B // 2
    r = lax.axis_index("row")
    b = lax.axis_index("bus")
    core = lax.rem(b, 2)
    zi = lax.div(b, 2)
    mrows, cols = mon_ref.shape
    orows = out_ref.shape[0]
    each = BLK // R
    cq = cols // R
    nblk_o, nblk_m = orows // each, mrows // each
    nblk = nblk_m + nblk_o
    n_sent = (R - 1) * (mrows + orows)
    kl = mid_ref.shape[1]
    kc = kl * R // B
    def row_dev(q):
        return {"row": q}

    def z_dev(q):
        return {"bus": q * 2 + core}

    pair_dev = {"bus": zi * 2 + (1 - core)}
    barrier = pltpu.get_barrier_semaphore()
    for d in range(1, R):
        pl.semaphore_signal(barrier, inc=1, device_id=row_dev(lax.rem(r + d, R)), device_id_type=MESH)
    for d in range(1, Z):
        pl.semaphore_signal(barrier, inc=1, device_id=z_dev(lax.rem(zi + d, Z)), device_id_type=MESH)
    pl.semaphore_signal(barrier, inc=1, device_id=pair_dev, device_id_type=MESH)
    loads = []
    for i, (src, dst) in enumerate(((w_hbm, w_ref), (table_hbm, table_ref), (mid_hbm, mid_ref),
                                    (oid_hbm, oid_ref), (lid_hbm, lid_ref))):
        c = pltpu.make_async_copy(src, dst, small.at[i])
        c.start()
        loads.append(c)
    pl.semaphore_wait(barrier, R - 1 + Z - 1 + 1)

    def source(k, q):
        ref, k = (out_ref, k) if k < nblk_o else (mon_ref, k - nblk_o)
        return ref.at[k * each:(k + 1) * each, pl.ds(pl.multiple_of(q * cq, 128), cq)]

    def target(k):
        return x.at[pl.ds(pl.multiple_of(k * BLK + r * each, each), each), :]

    def send_ids():
        for i, src in enumerate((mid_hbm, oid_hbm, lid_hbm)):
            for d in range(1, R):
                send(src, ids.at[i, r], i_s, i_r, row_dev(lax.rem(r + d, R)))
            pltpu.make_async_copy(src, ids.at[i, r], i_r).start()

    for k in range(nblk):
        for d in range(1, R):
            q = lax.rem(r + d, R)
            send(source(k, q), target(k), x_s, x_r.at[k], row_dev(q))
        pltpu.make_async_copy(source(k, r), target(k), x_r.at[k]).start()
        if k == 0:
            send_ids()
    for c in loads:
        c.wait()

    entries = table_ref.shape[1]
    for e in range(0, entries, 128):
        tt[e:e + 128, :] = down(table_ref[:, e:e + 128])
    c_row = down(factors(lid_ref[...], tt, entries))
    oid_t = down(oid_ref[...].astype(F32)).astype(jnp.int32)
    mid_t = down(mid_ref[...].astype(F32)).astype(jnp.int32)
    for k in range(nblk):
        for e in range(0, BLK, 128):
            at = slice(k * BLK + e, k * BLK + e + 128)
            if k < nblk_o:
                brow[:, at] = select(oid_t, (k, e), each, orows, 1, (kl, 128))
            else:
                brow[:, at] = select(mid_t, (k - nblk_o, e), each, mrows, 1, (kl, 128))
    scale = w_ref[:, pl.ds(pl.multiple_of(r * cq, 128), cq)] * (1.0 / nb_all)

    z_axis, row_axis = (Z, zi, z_dev), (R, r, row_dev)
    streams, at = [], 0
    for blocks, direct in plan(nblk):
        kind, n = (Direct, 7) if direct else (Staged, 11)
        streams.append(kind(rest[at:at + n], blocks, core, pair_dev, (z_axis, row_axis)))
        at += n

    def arrive(k):
        rows = slice(k * BLK, (k + 1) * BLK)
        arrived(x.at[rows, :], x_r.at[k])
        v = x[rows, :].astype(F32) * scale
        h = v.astype(BF16)
        xw[k, :BLK, :] = h
        xw[k, BLK:, :] = (v - h.astype(F32)).astype(BF16)

    def begin(stream):
        for k in stream.blocks:
            arrive(k)
            if len(stream.blocks) == 1 and (k + 1) * BLK == 2 * stream.H and stream.H % BLK == 0:
                stream.strip_half(k, x, xw, 1 - core)
                stream.at = 2 * stream.H
                stream.pair_start()
                stream.strip_half(k, x, xw, core)
                return
            stream.strip(k, x, xw)
        stream.pair_start()

    s1, s2, s3, s4 = streams
    begin(s1)
    s1.one_start()
    begin(s2)
    s2.one_start()
    s1.two_start()
    begin(s3)
    s3.one_start()
    begin(s4)
    s2.two_start()
    s4.one_start()

    arrived(ids, i_r)
    owner = lax.div(b * kc, kl)
    begin = pl.multiple_of(lax.rem(b * kc, kl), 128)
    mid_c = ids[0, owner, :, pl.ds(begin, kc)]
    oid_c = ids[1, owner, :, pl.ds(begin, kc)]
    c_col = factors(ids[2, owner, :, pl.ds(begin, kc)], tt, entries)
    bcol = [select(oid_c, (k, 0), each, orows, 0, (BLK, kc)) for k in range(nblk_o)]
    bcol += [select(mid_c, (k, 0), each, mrows, 0, (BLK, kc)) for k in range(nblk_m)]

    t_o[...] = jnp.zeros_like(t_o)
    t_m[...] = jnp.zeros_like(t_m)
    cut = nblk_o * BLK

    def times(v, cols_of):
        total = None
        for p in split(v):
            total = dot(p, cols_of) if total is None else total + dot(p, cols_of)
        return total

    def gather(stream):
        at = 0
        both = stream.whole()
        for k in stream.blocks:
            m = (k + 1) * BLK
            strip = both[at:at + m, :]
            at += m
            t = t_o if k < nblk_o else t_m
            t[:m, :] = t[:m, :] + times(strip, bcol[k])
            rows = slice(k * BLK, m)
            above = min(k * BLK, cut)
            if above > 0:
                part = jnp.concatenate(bcol[:above // BLK], axis=0)
                t_o[rows, :] = t_o[rows, :] + times(strip[:above, :].T, part)
            if k * BLK > cut:
                part = jnp.concatenate(bcol[nblk_o:k], axis=0)
                t_m[rows, :] = t_m[rows, :] + times(strip[cut:k * BLK, :].T, part)

    s1.back_start()
    s2.back_start()
    s3.back_start()
    s4.back_start()
    s1.spread_rest()
    s2.spread_rest()
    arrived(x.at[:n_sent, :], x_s)
    arrived(ids.at[:, :R - 1], i_s)
    for stream in streams:
        stream.settle()
    s3.pair_back()
    s1.pair_back()
    s2.pair_back()
    gather(s3)
    s4.pair_back()
    gather(s1)
    gather(s2)
    for stream in streams[:-1]:
        stream.finish()
    gather(s4)
    t = t_m[...] + t_o[...] * c_col
    t_hi, t_lo = split(t)
    step = kl // 4
    for at in range(0, kl, step):
        rows = slice(at, at + step)
        g_o = dot(brow[rows, :cut], t_hi[:cut, :]) + dot(brow[rows, :cut], t_lo[:cut, :])
        g_m = dot(brow[rows, cut:], t_hi[cut:, :]) + dot(brow[rows, cut:], t_lo[cut:, :])
        gram[rows, :] = g_m + g_o * jnp.concatenate([c_row[rows, :]] * (kc // 128), axis=1)
        pltpu.make_async_copy(gram.at[rows, :], gram_ref.at[rows, :], g_s).start()
    arrived(gram, g_s)
    s4.finish()


def plan(nblk):
    cuts = [0, nblk // 2, nblk - 2, nblk - 1, nblk]
    return [(range(a, b), i > 1) for i, (a, b) in enumerate(zip(cuts, cuts[1:]))]


def solution(mesh):
    R, B = mesh.shape["row"], mesh.shape["bus"]
    Z = B // 2

    def stream_scratch(blocks, n1, n2):
        unit = 8 * R * B
        packed = -(-(blocks * BLK) // unit) * unit
        H = packed // 2
        h1 = H // n1
        pz = h1 // n2
        dma = pltpu.SemaphoreType.DMA
        return [
            pltpu.VMEM((packed, BLK), F32),
            pltpu.VMEM((H, BLK), F32),
            pltpu.VMEM((H, BLK), F32),
            pltpu.VMEM((n1, h1, BLK), I16),
            pltpu.VMEM((n1 - 1, h1, BLK), I16),
            pltpu.VMEM((h1, BLK), F32),
            pltpu.VMEM((n2, pz, BLK), I16),
            pltpu.VMEM((n2 - 1, pz, BLK), I16),
            pltpu.VMEM((2, n1 * n2, pz, BLK), I16),
            dma((STAGED,)), dma((Z - 1,)),
        ]

    def direct_scratch(blocks):
        unit = 8 * R * B
        packed = -(-(blocks * BLK) // unit) * unit
        H = packed // 2
        n = R * Z
        dma = pltpu.SemaphoreType.DMA
        return [
            pltpu.VMEM((packed, BLK), F32),
            pltpu.VMEM((H, BLK), F32),
            pltpu.VMEM((H, BLK), F32),
            pltpu.VMEM((n, H // n, BLK), I16),
            pltpu.VMEM((n - 1, H // n, BLK), I16),
            pltpu.VMEM((2, n, H // n, BLK), I16),
            dma((DIRECT,)),
        ]

    def local(monitored, outaged, bus_weight, lodf_table, mon_id, out_id, lodf_idx):
        mrows, cols = monitored.shape
        orows = outaged.shape[0]
        n = (mrows + orows) * R
        cq = cols // R
        nblk = n // BLK
        kl = mon_id.shape[0]
        kc = kl * R // B
        hbm = pl.BlockSpec(memory_space=pl.ANY)
        dma = pltpu.SemaphoreType.DMA
        streams = plan(nblk)
        return pl.pallas_call(
            functools.partial(kernel, (R, B, cols * B)),
            out_shape=jax.ShapeDtypeStruct((kl, kc), F32),
            in_specs=[hbm] * 7,
            out_specs=hbm,
            scratch_shapes=[
                pltpu.VMEM((1, cols), F32),
                pltpu.VMEM((1, lodf_table.shape[0]), F32),
                pltpu.VMEM((1, kl), jnp.int32),
                pltpu.VMEM((1, kl), jnp.int32),
                pltpu.VMEM((1, kl), jnp.int32),
                dma((5,)),
                pltpu.VMEM((n, cq), BF16),
                pltpu.VMEM((nblk, 2 * BLK, cq), BF16),
                pltpu.VMEM((lodf_table.shape[0], 128), F32),
                pltpu.VMEM((3, R, 1, kl), jnp.int32),
                pltpu.VMEM((kl, n), BF16),
                pltpu.VMEM((n, kc), F32),
                pltpu.VMEM((n, kc), F32),
                dma, dma((nblk,)), dma, dma, pltpu.VMEM((kl, kc), F32), dma,
            ] + [
                ref for blocks, direct in streams
                for ref in (direct_scratch(sum(k + 1 for k in blocks)) if direct else
                            stream_scratch(sum(k + 1 for k in blocks), Z, R))
            ],
            compiler_params=pltpu.CompilerParams(
                collective_id=0, has_side_effects=True, vmem_limit_bytes=60 * 1024 * 1024),
        )(monitored, outaged, bus_weight[None, :], lodf_table[None, :],
          mon_id[None, :], out_id[None, :], lodf_idx[None, :])

    in_specs = (P("row", "bus"), P("row", "bus"), P("bus"), P(), P("row"), P("row"), P("row"))
    return jax.shard_map(local, mesh=mesh, in_specs=in_specs, out_specs=P("row", "bus"), check_vma=False)
```

```python
import functools
import math

import jax
import jax.numpy as jnp
from jax import lax
from jax.experimental import pallas as pl
from jax.experimental.pallas import tpu as pltpu
from jax.sharding import PartitionSpec as P

BLK = 128
TINY = 1e-30
BOUND = 6.0 * 6.0 * 4.0 * 1.01
F32 = jnp.float32
BF16 = jnp.bfloat16
I16 = jnp.int16
STAGED, DIRECT = 11, 8
MESH = pl.DeviceIdType.MESH


def split(v):
    a = v.astype(BF16)
    return a, (v - a.astype(F32)).astype(BF16)


def dot(a, b):
    return jnp.dot(a, b, preferred_element_type=F32)


def dot_t(a, b):
    return lax.dot_general(a, b, (((1,), (1,)), ((), ())), preferred_element_type=F32)


def encode(v, bound):
    u = jnp.log2(jnp.maximum(jnp.abs(v), TINY)) * (1 / 16) + math.log2(32767.0 / bound ** (1 / 16))
    u = jnp.minimum(jnp.exp2(u) + 0.5, 32767.0)
    return jnp.where(v < 0, -u, u).astype(jnp.int32).astype(I16)


def decode(q, bound):
    f = q.astype(jnp.int32).astype(F32) * (bound ** (1 / 16) / 32767.0)
    u = f
    for _ in range(4):
        u = u * u
    return jnp.where(f < 0, -u, u)


def down(lanes):
    n = lanes.shape[1]
    return jnp.broadcast_to(lanes, (128, n)).T


def factors(idx, table_t, entries):
    n = idx.shape[1]
    parts = []
    for lo in range(0, n, 128):
        total = jnp.zeros((1, 128), F32)
        for e in range(0, entries, 128):
            rows = lax.broadcasted_iota(jnp.int32, (128, 128), 0) + e
            hit = jnp.where(rows == idx[:, lo:lo + 128], table_t[e:e + 128, :], 0.0)
            total = total + jnp.sum(hit, axis=0, keepdims=True)
        parts.append(total)
    return jnp.concatenate(parts, axis=1)


def arrived(ref, sem):
    pltpu.make_async_copy(ref, ref, sem).wait()


def send(src, dst, s, r, dev):
    pltpu.make_async_remote_copy(
        src_ref=src, dst_ref=dst, send_sem=s, recv_sem=r, device_id=dev, device_id_type=MESH).start()


class Stream:
    def setup(self, blocks, core, other):
        self.blocks = blocks
        self.core, self.other = core, other
        self.H = self.gp.shape[0] // 2
        self.at = 0

    def strip(self, k, x, xw):
        m = (k + 1) * BLK
        both = dot_t(x[:m, :], xw[k])
        self.gp[self.at:self.at + m, :] = both[:, :BLK] + both[:, BLK:]
        self.at += m

    def strip_half(self, k, x, xw, core):
        rows = pl.ds(pl.multiple_of(core * self.H, BLK), self.H)
        both = dot_t(x[rows, :], xw[k])
        self.gp[rows, :] = both[:, :BLK] + both[:, BLK:]

    def rows(self, start, count):
        return pl.ds(pl.multiple_of(start, 8), count)

    def half(self, core):
        return self.gp.at[self.rows(core * self.H, self.H), :]

    def pair_start(self):
        if self.gp.shape[0] > self.at:
            self.gp[self.at:, :] = jnp.zeros((self.gp.shape[0] - self.at, BLK), F32)
        send(self.half(1 - self.core), self.cbuf, self.cs, self.cr, self.other)

    def pair_sum(self):
        arrived(self.cbuf, self.cr)
        total = self.half(self.core)[...] + self.cbuf[...]
        self.acc[...] = total
        self.e1[...] = encode(total, BOUND).reshape(self.e1.shape)

    def pair_back(self):
        ref = self.full.at[self.core]
        send(ref, ref, self.ds, self.dr, self.other)

    def whole(self):
        arrived(self.full.at[1 - self.core], self.dr)
        return decode(self.full[...], BOUND).reshape(self.gp.shape)


class Staged(Stream):
    def __init__(self, refs, blocks, core, other, axes):
        (self.gp, self.cbuf, self.acc, self.e1, self.b1, self.s1, self.e2, self.b2, self.full, sem, self.zr) = refs
        (self.cs, self.cr, self.p1s, self.p1r, self.p2s, self.p2r,
         self.a1s, self.a2s, self.a2r, self.ds, self.dr) = [sem.at[i] for i in range(STAGED)]
        self.setup(blocks, core, other)
        (self.Z, self.zi, self.zdev), (self.R, self.r, self.rdev) = axes
        self.h1 = self.H // self.Z
        self.pz = self.h1 // self.R

    def one_start(self):
        self.pair_sum()
        for d in range(1, self.Z):
            q = lax.rem(self.zi + d, self.Z)
            send(self.e1.at[q], self.b1.at[d - 1], self.p1s, self.p1r, self.zdev(q))

    def two_start(self):
        arrived(self.b1, self.p1r)
        total = self.acc[self.rows(self.zi * self.h1, self.h1), :]
        for d in range(1, self.Z):
            total = total + decode(self.b1[d - 1], BOUND)
        self.s1[...] = total
        self.e2[...] = encode(total, BOUND).reshape(self.e2.shape)
        for d in range(1, self.R):
            q = lax.rem(self.r + d, self.R)
            send(self.e2.at[q], self.b2.at[d - 1], self.p2s, self.p2r, self.rdev(q))

    def piece(self, z):
        return self.full.at[self.core, z * self.R + self.r]

    def back_start(self):
        arrived(self.b2, self.p2r)
        total = self.s1[self.rows(self.r * self.pz, self.pz), :]
        for d in range(1, self.R):
            total = total + decode(self.b2[d - 1], BOUND)
        ref = self.piece(self.zi)
        ref[...] = encode(total, BOUND)
        for d in range(1, self.Z):
            send(ref, ref, self.a1s, self.zr.at[d - 1], self.zdev(lax.rem(self.zi + d, self.Z)))
        self.spread(ref)

    def spread(self, ref):
        for d in range(1, self.R):
            send(ref, ref, self.a2s, self.a2r, self.rdev(lax.rem(self.r + d, self.R)))

    def spread_rest(self):
        for e in range(1, self.Z):
            ref = self.piece(lax.rem(self.zi + self.Z - e, self.Z))
            arrived(ref, self.zr.at[e - 1])
            self.spread(ref)

    def pair_back(self):
        arrived(self.full.at[self.core, :self.Z * (self.R - 1)], self.a2r)
        super().pair_back()

    def settle(self):
        arrived(self.cbuf, self.cs)
        arrived(self.b1, self.p1s)
        arrived(self.b2, self.p2s)

    def finish(self):
        arrived(self.full.at[0, :self.Z - 1], self.a1s)
        arrived(self.full.at[0, :self.Z * (self.R - 1)], self.a2s)
        arrived(self.full.at[0], self.ds)


class Direct(Stream):
    def __init__(self, refs, blocks, core, other, axes):
        self.gp, self.cbuf, self.acc, self.e1, self.b1, self.full, sem = refs
        (self.cs, self.cr, self.p1s, self.p1r, self.a1s, self.a1r, self.ds, self.dr) = [
            sem.at[i] for i in range(DIRECT)]
        self.setup(blocks, core, other)
        (self.Z, self.zi, _), (self.R, self.r, _) = axes
        self.N = self.Z * self.R
        self.pz = self.H // self.N

    def peers(self):
        for j in sorted(range(1, self.N), key=lambda j: (-min(j // self.R, self.Z - j // self.R), -(j % self.R))):
            z = lax.rem(self.zi + j // self.R, self.Z)
            r = lax.rem(self.r + j % self.R, self.R)
            yield j - 1, z * self.R + r, {"row": r, "bus": z * 2 + self.core}

    def one_start(self):
        self.pair_sum()
        for j, at, dev in self.peers():
            send(self.e1.at[at], self.b1.at[j], self.p1s, self.p1r, dev)

    def back_start(self):
        arrived(self.b1, self.p1r)
        me = self.zi * self.R + self.r
        total = self.acc[self.rows(me * self.pz, self.pz), :]
        for j in range(self.N - 1):
            total = total + decode(self.b1[j], BOUND)
        ref = self.full.at[self.core, me]
        ref[...] = encode(total, BOUND)
        for _, _, dev in self.peers():
            send(ref, ref, self.a1s, self.a1r, dev)

    def pair_back(self):
        arrived(self.full.at[self.core, :self.N - 1], self.a1r)
        super().pair_back()

    def settle(self):
        arrived(self.cbuf, self.cs)
        arrived(self.b1, self.p1s)

    def finish(self):
        arrived(self.full.at[0, :self.N - 1], self.a1s)
        arrived(self.full.at[0], self.ds)


def select(ids, block, rows_each, dev_rows, axis, shape):
    p = lax.broadcasted_iota(jnp.int32, shape, axis)
    if axis == 1:
        p = p + block[1]
    shift = rows_each.bit_length() - 1
    line = lax.shift_right_logical(p, jnp.full(shape, shift, jnp.int32)) * (dev_rows - rows_each) + p
    return jnp.where(ids == line + block[0] * rows_each, 1.0, 0.0).astype(BF16)


def kernel(dims, mon_ref, out_ref, w_hbm, table_hbm, mid_hbm, oid_hbm, lid_hbm,
           gram_ref, w_ref, table_ref, mid_ref, oid_ref, lid_ref, small, x, xw, tt, ids, brow, t_o, t_m, x_s, x_r, i_s, i_r, gram, g_s, *rest):
    R, B, nb_all = dims
    Z = B // 2
    r = lax.axis_index("row")
    b = lax.axis_index("bus")
    core = lax.rem(b, 2)
    zi = lax.div(b, 2)
    mrows, cols = mon_ref.shape
    orows = out_ref.shape[0]
    each = BLK // R
    cq = cols // R
    nblk_o, nblk_m = orows // each, mrows // each
    nblk = nblk_m + nblk_o
    n_sent = (R - 1) * (mrows + orows)
    kl = mid_ref.shape[1]
    kc = kl * R // B
    def row_dev(q):
        return {"row": q}

    def z_dev(q):
        return {"bus": q * 2 + core}

    pair_dev = {"bus": zi * 2 + (1 - core)}
    barrier = pltpu.get_barrier_semaphore()
    for d in range(1, R):
        pl.semaphore_signal(barrier, inc=1, device_id=row_dev(lax.rem(r + d, R)), device_id_type=MESH)
    for d in range(1, Z):
        pl.semaphore_signal(barrier, inc=1, device_id=z_dev(lax.rem(zi + d, Z)), device_id_type=MESH)
    pl.semaphore_signal(barrier, inc=1, device_id=pair_dev, device_id_type=MESH)
    loads = []
    for i, (src, dst) in enumerate(((w_hbm, w_ref), (table_hbm, table_ref), (mid_hbm, mid_ref),
                                    (oid_hbm, oid_ref), (lid_hbm, lid_ref))):
        c = pltpu.make_async_copy(src, dst, small.at[i])
        c.start()
        loads.append(c)
    pl.semaphore_wait(barrier, R - 1 + Z - 1 + 1)

    def source(k, q):
        ref, k = (out_ref, k) if k < nblk_o else (mon_ref, k - nblk_o)
        return ref.at[k * each:(k + 1) * each, pl.ds(pl.multiple_of(q * cq, 128), cq)]

    def target(k):
        return x.at[pl.ds(pl.multiple_of(k * BLK + r * each, each), each), :]

    def send_ids():
        for i, src in enumerate((mid_hbm, oid_hbm, lid_hbm)):
            for d in range(1, R):
                send(src, ids.at[i, r], i_s, i_r, row_dev(lax.rem(r + d, R)))
            pltpu.make_async_copy(src, ids.at[i, r], i_r).start()

    for k in range(nblk):
        for d in range(1, R):
            q = lax.rem(r + d, R)
            send(source(k, q), target(k), x_s, x_r.at[k], row_dev(q))
        pltpu.make_async_copy(source(k, r), target(k), x_r.at[k]).start()
        if k == 0:
            send_ids()
    for c in loads:
        c.wait()

    entries = table_ref.shape[1]
    for e in range(0, entries, 128):
        tt[e:e + 128, :] = down(table_ref[:, e:e + 128])
    c_row = down(factors(lid_ref[...], tt, entries))
    oid_t = down(oid_ref[...].astype(F32)).astype(jnp.int32)
    mid_t = down(mid_ref[...].astype(F32)).astype(jnp.int32)
    for k in range(nblk):
        for e in range(0, BLK, 128):
            at = slice(k * BLK + e, k * BLK + e + 128)
            if k < nblk_o:
                brow[:, at] = select(oid_t, (k, e), each, orows, 1, (kl, 128))
            else:
                brow[:, at] = select(mid_t, (k - nblk_o, e), each, mrows, 1, (kl, 128))
    scale = w_ref[:, pl.ds(pl.multiple_of(r * cq, 128), cq)] * (1.0 / nb_all)

    z_axis, row_axis = (Z, zi, z_dev), (R, r, row_dev)
    streams, at = [], 0
    for blocks, direct in plan(nblk):
        kind, n = (Direct, 7) if direct else (Staged, 11)
        streams.append(kind(rest[at:at + n], blocks, core, pair_dev, (z_axis, row_axis)))
        at += n

    def arrive(k):
        rows = slice(k * BLK, (k + 1) * BLK)
        arrived(x.at[rows, :], x_r.at[k])
        v = x[rows, :].astype(F32) * scale
        h = v.astype(BF16)
        xw[k, :BLK, :] = h
        xw[k, BLK:, :] = (v - h.astype(F32)).astype(BF16)

    def begin(stream):
        for k in stream.blocks:
            arrive(k)
            if len(stream.blocks) == 1 and (k + 1) * BLK == 2 * stream.H and stream.H % BLK == 0:
                stream.strip_half(k, x, xw, 1 - core)
                stream.at = 2 * stream.H
                stream.pair_start()
                stream.strip_half(k, x, xw, core)
                return
            stream.strip(k, x, xw)
        stream.pair_start()

    s1, s2, s3, s4 = streams
    begin(s1)
    s1.one_start()
    begin(s2)
    s2.one_start()
    s1.two_start()
    begin(s3)
    s3.one_start()
    begin(s4)
    s2.two_start()
    s4.one_start()

    arrived(ids, i_r)
    owner = lax.div(b * kc, kl)
    begin = pl.multiple_of(lax.rem(b * kc, kl), 128)
    mid_c = ids[0, owner, :, pl.ds(begin, kc)]
    oid_c = ids[1, owner, :, pl.ds(begin, kc)]
    c_col = factors(ids[2, owner, :, pl.ds(begin, kc)], tt, entries)
    bcol = [select(oid_c, (k, 0), each, orows, 0, (BLK, kc)) for k in range(nblk_o)]
    bcol += [select(mid_c, (k, 0), each, mrows, 0, (BLK, kc)) for k in range(nblk_m)]

    t_o[...] = jnp.zeros_like(t_o)
    t_m[...] = jnp.zeros_like(t_m)
    cut = nblk_o * BLK

    def times(v, cols_of):
        a, b = split(v)
        return dot(jnp.concatenate([a, b], axis=1), jnp.concatenate([cols_of, cols_of], axis=0))

    def gather(stream):
        at = 0
        both = stream.whole()
        for k in stream.blocks:
            m = (k + 1) * BLK
            strip = both[at:at + m, :]
            at += m
            t = t_o if k < nblk_o else t_m
            t[:m, :] = t[:m, :] + times(strip, bcol[k])
            rows = slice(k * BLK, m)
            above = min(k * BLK, cut)
            if above > 0:
                part = jnp.concatenate(bcol[:above // BLK], axis=0)
                t_o[rows, :] = t_o[rows, :] + times(strip[:above, :].T, part)
            if k * BLK > cut:
                part = jnp.concatenate(bcol[nblk_o:k], axis=0)
                t_m[rows, :] = t_m[rows, :] + times(strip[cut:k * BLK, :].T, part)

    s1.back_start()
    s2.back_start()
    s3.back_start()
    s4.back_start()
    s1.spread_rest()
    s2.spread_rest()
    arrived(x.at[:n_sent, :], x_s)
    arrived(ids.at[:, :R - 1], i_s)
    for stream in streams:
        stream.settle()
    s3.pair_back()
    s1.pair_back()
    s2.pair_back()
    gather(s3)
    s4.pair_back()
    gather(s1)
    gather(s2)
    for stream in streams[:-1]:
        stream.finish()
    gather(s4)
    t = t_m[...] + t_o[...] * c_col
    t_hi, t_lo = split(t)
    step = kl // 4
    for at in range(0, kl, step):
        rows = slice(at, at + step)
        g_o = dot(brow[rows, :cut], t_hi[:cut, :]) + dot(brow[rows, :cut], t_lo[:cut, :])
        g_m = dot(brow[rows, cut:], t_hi[cut:, :]) + dot(brow[rows, cut:], t_lo[cut:, :])
        gram[rows, :] = g_m + g_o * jnp.concatenate([c_row[rows, :]] * (kc // 128), axis=1)
        pltpu.make_async_copy(gram.at[rows, :], gram_ref.at[rows, :], g_s).start()
    arrived(gram, g_s)
    s4.finish()


def plan(nblk):
    cuts = [0, nblk // 2, nblk - 2, nblk - 1, nblk]
    return [(range(a, b), i > 1) for i, (a, b) in enumerate(zip(cuts, cuts[1:]))]


def solution(mesh):
    R, B = mesh.shape["row"], mesh.shape["bus"]
    Z = B // 2

    def stream_scratch(blocks, n1, n2):
        unit = 8 * R * B
        packed = -(-(blocks * BLK) // unit) * unit
        H = packed // 2
        h1 = H // n1
        pz = h1 // n2
        dma = pltpu.SemaphoreType.DMA
        return [
            pltpu.VMEM((packed, BLK), F32),
            pltpu.VMEM((H, BLK), F32),
            pltpu.VMEM((H, BLK), F32),
            pltpu.VMEM((n1, h1, BLK), I16),
            pltpu.VMEM((n1 - 1, h1, BLK), I16),
            pltpu.VMEM((h1, BLK), F32),
            pltpu.VMEM((n2, pz, BLK), I16),
            pltpu.VMEM((n2 - 1, pz, BLK), I16),
            pltpu.VMEM((2, n1 * n2, pz, BLK), I16),
            dma((STAGED,)), dma((Z - 1,)),
        ]

    def direct_scratch(blocks):
        unit = 8 * R * B
        packed = -(-(blocks * BLK) // unit) * unit
        H = packed // 2
        n = R * Z
        dma = pltpu.SemaphoreType.DMA
        return [
            pltpu.VMEM((packed, BLK), F32),
            pltpu.VMEM((H, BLK), F32),
            pltpu.VMEM((H, BLK), F32),
            pltpu.VMEM((n, H // n, BLK), I16),
            pltpu.VMEM((n - 1, H // n, BLK), I16),
            pltpu.VMEM((2, n, H // n, BLK), I16),
            dma((DIRECT,)),
        ]

    def local(monitored, outaged, bus_weight, lodf_table, mon_id, out_id, lodf_idx):
        mrows, cols = monitored.shape
        orows = outaged.shape[0]
        n = (mrows + orows) * R
        cq = cols // R
        nblk = n // BLK
        kl = mon_id.shape[0]
        kc = kl * R // B
        hbm = pl.BlockSpec(memory_space=pl.ANY)
        dma = pltpu.SemaphoreType.DMA
        streams = plan(nblk)
        return pl.pallas_call(
            functools.partial(kernel, (R, B, cols * B)),
            out_shape=jax.ShapeDtypeStruct((kl, kc), F32),
            in_specs=[hbm] * 7,
            out_specs=hbm,
            scratch_shapes=[
                pltpu.VMEM((1, cols), F32),
                pltpu.VMEM((1, lodf_table.shape[0]), F32),
                pltpu.VMEM((1, kl), jnp.int32),
                pltpu.VMEM((1, kl), jnp.int32),
                pltpu.VMEM((1, kl), jnp.int32),
                dma((5,)),
                pltpu.VMEM((n, cq), BF16),
                pltpu.VMEM((nblk, 2 * BLK, cq), BF16),
                pltpu.VMEM((lodf_table.shape[0], 128), F32),
                pltpu.VMEM((3, R, 1, kl), jnp.int32),
                pltpu.VMEM((kl, n), BF16),
                pltpu.VMEM((n, kc), F32),
                pltpu.VMEM((n, kc), F32),
                dma, dma((nblk,)), dma, dma, pltpu.VMEM((kl, kc), F32), dma,
            ] + [
                ref for blocks, direct in streams
                for ref in (direct_scratch(sum(k + 1 for k in blocks)) if direct else
                            stream_scratch(sum(k + 1 for k in blocks), Z, R))
            ],
            compiler_params=pltpu.CompilerParams(
                collective_id=0, has_side_effects=True, vmem_limit_bytes=60 * 1024 * 1024),
        )(monitored, outaged, bus_weight[None, :], lodf_table[None, :],
          mon_id[None, :], out_id[None, :], lodf_idx[None, :])

    in_specs = (P("row", "bus"), P("row", "bus"), P("bus"), P(), P("row"), P("row"), P("row"))
    return jax.shard_map(local, mesh=mesh, in_specs=in_specs, out_specs=P("row", "bus"), check_vma=False)
```

```python
import functools
import math

import jax
import jax.numpy as jnp
from jax import lax
from jax.experimental import pallas as pl
from jax.experimental.pallas import tpu as pltpu
from jax.sharding import PartitionSpec as P

BLK = 128
TINY = 1e-30
BOUND = 6.0 * 6.0 * 4.0 * 1.01
F32 = jnp.float32
BF16 = jnp.bfloat16
I16 = jnp.int16
STAGED, DIRECT = 11, 8
MESH = pl.DeviceIdType.MESH


def split(v):
    a = v.astype(BF16)
    return a, (v - a.astype(F32)).astype(BF16)


def dot(a, b):
    return jnp.dot(a, b, preferred_element_type=F32)


def dot_t(a, b):
    return lax.dot_general(a, b, (((1,), (1,)), ((), ())), preferred_element_type=F32)


def encode(v, bound):
    u = jnp.log2(jnp.maximum(jnp.abs(v), TINY)) * (1 / 16) + math.log2(32767.0 / bound ** (1 / 16))
    u = jnp.minimum(jnp.exp2(u) + 0.5, 32767.0)
    return jnp.where(v < 0, -u, u).astype(jnp.int32).astype(I16)


def decode(q, bound):
    f = q.astype(jnp.int32).astype(F32) * (bound ** (1 / 16) / 32767.0)
    u = f
    for _ in range(4):
        u = u * u
    return jnp.where(f < 0, -u, u)


def down(lanes):
    n = lanes.shape[1]
    return jnp.broadcast_to(lanes, (128, n)).T


def factors(idx, table_t, entries):
    n = idx.shape[1]
    parts = []
    for lo in range(0, n, 128):
        total = jnp.zeros((1, 128), F32)
        for e in range(0, entries, 128):
            rows = lax.broadcasted_iota(jnp.int32, (128, 128), 0) + e
            hit = jnp.where(rows == idx[:, lo:lo + 128], table_t[e:e + 128, :], 0.0)
            total = total + jnp.sum(hit, axis=0, keepdims=True)
        parts.append(total)
    return jnp.concatenate(parts, axis=1)


def arrived(ref, sem):
    pltpu.make_async_copy(ref, ref, sem).wait()


def send(src, dst, s, r, dev):
    pltpu.make_async_remote_copy(
        src_ref=src, dst_ref=dst, send_sem=s, recv_sem=r, device_id=dev, device_id_type=MESH).start()


class Stream:
    def setup(self, blocks, core, other):
        self.blocks = blocks
        self.core, self.other = core, other
        self.H = self.gp.shape[0] // 2
        self.at = 0

    def strip(self, k, x, xw):
        m = (k + 1) * BLK
        both = dot_t(x[:m, :], xw[k])
        self.gp[self.at:self.at + m, :] = both[:, :BLK] + both[:, BLK:]
        self.at += m

    def strip_half(self, k, x, xw, core):
        rows = pl.ds(pl.multiple_of(core * self.H, BLK), self.H)
        both = dot_t(x[rows, :], xw[k])
        self.gp[rows, :] = both[:, :BLK] + both[:, BLK:]

    def rows(self, start, count):
        return pl.ds(pl.multiple_of(start, 8), count)

    def half(self, core):
        return self.gp.at[self.rows(core * self.H, self.H), :]

    def pair_start(self):
        if self.gp.shape[0] > self.at:
            self.gp[self.at:, :] = jnp.zeros((self.gp.shape[0] - self.at, BLK), F32)
        send(self.half(1 - self.core), self.cbuf, self.cs, self.cr, self.other)

    def pair_sum(self):
        arrived(self.cbuf, self.cr)
        total = self.half(self.core)[...] + self.cbuf[...]
        self.acc[...] = total
        self.e1[...] = encode(total, BOUND).reshape(self.e1.shape)

    def pair_back(self):
        ref = self.full.at[self.core]
        send(ref, ref, self.ds, self.dr, self.other)

    def whole(self):
        arrived(self.full.at[1 - self.core], self.dr)
        return decode(self.full[...], BOUND).reshape(self.gp.shape)


class Staged(Stream):
    def __init__(self, refs, blocks, core, other, axes):
        (self.gp, self.cbuf, self.acc, self.e1, self.b1, self.s1, self.e2, self.b2, self.full, sem, self.zr) = refs
        (self.cs, self.cr, self.p1s, self.p1r, self.p2s, self.p2r,
         self.a1s, self.a2s, self.a2r, self.ds, self.dr) = [sem.at[i] for i in range(STAGED)]
        self.setup(blocks, core, other)
        (self.Z, self.zi, self.zdev), (self.R, self.r, self.rdev) = axes
        self.h1 = self.H // self.Z
        self.pz = self.h1 // self.R

    def one_start(self):
        self.pair_sum()
        for d in range(1, self.Z):
            q = lax.rem(self.zi + d, self.Z)
            send(self.e1.at[q], self.b1.at[d - 1], self.p1s, self.p1r, self.zdev(q))

    def two_start(self):
        arrived(self.b1, self.p1r)
        total = self.acc[self.rows(self.zi * self.h1, self.h1), :]
        for d in range(1, self.Z):
            total = total + decode(self.b1[d - 1], BOUND)
        self.s1[...] = total
        self.e2[...] = encode(total, BOUND).reshape(self.e2.shape)
        for d in range(1, self.R):
            q = lax.rem(self.r + d, self.R)
            send(self.e2.at[q], self.b2.at[d - 1], self.p2s, self.p2r, self.rdev(q))

    def piece(self, z):
        return self.full.at[self.core, z * self.R + self.r]

    def back_start(self):
        arrived(self.b2, self.p2r)
        total = self.s1[self.rows(self.r * self.pz, self.pz), :]
        for d in range(1, self.R):
            total = total + decode(self.b2[d - 1], BOUND)
        ref = self.piece(self.zi)
        ref[...] = encode(total, BOUND)
        for d in range(1, self.Z):
            send(ref, ref, self.a1s, self.zr.at[d - 1], self.zdev(lax.rem(self.zi + d, self.Z)))
        self.spread(ref)

    def spread(self, ref):
        for d in range(1, self.R):
            send(ref, ref, self.a2s, self.a2r, self.rdev(lax.rem(self.r + d, self.R)))

    def spread_rest(self):
        for e in range(1, self.Z):
            ref = self.piece(lax.rem(self.zi + self.Z - e, self.Z))
            arrived(ref, self.zr.at[e - 1])
            self.spread(ref)

    def pair_back(self):
        arrived(self.full.at[self.core, :self.Z * (self.R - 1)], self.a2r)
        super().pair_back()

    def settle(self):
        arrived(self.cbuf, self.cs)
        arrived(self.b1, self.p1s)
        arrived(self.b2, self.p2s)

    def finish(self):
        arrived(self.full.at[0, :self.Z - 1], self.a1s)
        arrived(self.full.at[0, :self.Z * (self.R - 1)], self.a2s)
        arrived(self.full.at[0], self.ds)


class Direct(Stream):
    def __init__(self, refs, blocks, core, other, axes):
        self.gp, self.cbuf, self.acc, self.e1, self.b1, self.full, sem = refs
        (self.cs, self.cr, self.p1s, self.p1r, self.a1s, self.a1r, self.ds, self.dr) = [
            sem.at[i] for i in range(DIRECT)]
        self.setup(blocks, core, other)
        (self.Z, self.zi, _), (self.R, self.r, _) = axes
        self.N = self.Z * self.R
        self.pz = self.H // self.N

    def peers(self):
        for j in sorted(range(1, self.N), key=lambda j: (-min(j // self.R, self.Z - j // self.R), -(j % self.R))):
            z = lax.rem(self.zi + j // self.R, self.Z)
            r = lax.rem(self.r + j % self.R, self.R)
            yield j - 1, z * self.R + r, {"row": r, "bus": z * 2 + self.core}

    def one_start(self):
        self.pair_sum()
        for j, at, dev in self.peers():
            send(self.e1.at[at], self.b1.at[j], self.p1s, self.p1r, dev)

    def back_start(self):
        arrived(self.b1, self.p1r)
        me = self.zi * self.R + self.r
        total = self.acc[self.rows(me * self.pz, self.pz), :]
        for j in range(self.N - 1):
            total = total + decode(self.b1[j], BOUND)
        ref = self.full.at[self.core, me]
        ref[...] = encode(total, BOUND)
        for _, _, dev in self.peers():
            send(ref, ref, self.a1s, self.a1r, dev)

    def pair_back(self):
        arrived(self.full.at[self.core, :self.N - 1], self.a1r)
        super().pair_back()

    def settle(self):
        arrived(self.cbuf, self.cs)
        arrived(self.b1, self.p1s)

    def finish(self):
        arrived(self.full.at[0, :self.N - 1], self.a1s)
        arrived(self.full.at[0], self.ds)


def select(ids, block, rows_each, dev_rows, axis, shape):
    p = lax.broadcasted_iota(jnp.int32, shape, axis)
    if axis == 1:
        p = p + block[1]
    shift = rows_each.bit_length() - 1
    line = lax.shift_right_logical(p, jnp.full(shape, shift, jnp.int32)) * (dev_rows - rows_each) + p
    return jnp.where(ids == line + block[0] * rows_each, 1.0, 0.0).astype(BF16)


def kernel(dims, mon_ref, out_ref, w_hbm, table_hbm, mid_hbm, oid_hbm, lid_hbm,
           gram_ref, w_ref, table_ref, small, x, xw, tt, ids, brow, t_o, t_m, x_s, x_r, i_s, i_r, gram, g_s, *rest):
    R, B, nb_all = dims
    Z = B // 2
    r = lax.axis_index("row")
    b = lax.axis_index("bus")
    core = lax.rem(b, 2)
    zi = lax.div(b, 2)
    mrows, cols = mon_ref.shape
    orows = out_ref.shape[0]
    each = BLK // R
    cq = cols // R
    nblk_o, nblk_m = orows // each, mrows // each
    nblk = nblk_m + nblk_o
    n_sent = (R - 1) * (mrows + orows)
    kl = mid_hbm.shape[1]
    kc = kl * R // B
    def row_dev(q):
        return {"row": q}

    def z_dev(q):
        return {"bus": q * 2 + core}

    pair_dev = {"bus": zi * 2 + (1 - core)}
    barrier = pltpu.get_barrier_semaphore()
    for d in range(1, R):
        pl.semaphore_signal(barrier, inc=1, device_id=row_dev(lax.rem(r + d, R)), device_id_type=MESH)
    for d in range(1, Z):
        pl.semaphore_signal(barrier, inc=1, device_id=z_dev(lax.rem(zi + d, Z)), device_id_type=MESH)
    pl.semaphore_signal(barrier, inc=1, device_id=pair_dev, device_id_type=MESH)
    loads = []
    for i, (src, dst) in enumerate(((w_hbm, w_ref), (table_hbm, table_ref))):
        c = pltpu.make_async_copy(src, dst, small.at[i])
        c.start()
        loads.append(c)
    pl.semaphore_wait(barrier, R - 1 + Z - 1 + 1)

    def source(k, q):
        ref, k = (out_ref, k) if k < nblk_o else (mon_ref, k - nblk_o)
        return ref.at[k * each:(k + 1) * each, pl.ds(pl.multiple_of(q * cq, 128), cq)]

    def target(k):
        return x.at[pl.ds(pl.multiple_of(k * BLK + r * each, each), each), :]

    def send_ids():
        for i, src in enumerate((mid_hbm, oid_hbm, lid_hbm)):
            for d in range(1, R):
                send(src, ids.at[i, r], i_s, i_r, row_dev(lax.rem(r + d, R)))
            pltpu.make_async_copy(src, ids.at[i, r], i_r).start()

    for k in range(nblk):
        for d in range(1, R):
            q = lax.rem(r + d, R)
            send(source(k, q), target(k), x_s, x_r.at[k], row_dev(q))
        pltpu.make_async_copy(source(k, r), target(k), x_r.at[k]).start()
        if k == 0:
            send_ids()
    for c in loads:
        c.wait()
    arrived(ids, i_r)

    entries = table_ref.shape[1]
    for e in range(0, entries, 128):
        tt[e:e + 128, :] = down(table_ref[:, e:e + 128])
    c_row = down(factors(ids[2, r], tt, entries))
    oid_t = down(ids[1, r].astype(F32)).astype(jnp.int32)
    mid_t = down(ids[0, r].astype(F32)).astype(jnp.int32)
    for k in range(nblk):
        for e in range(0, BLK, 128):
            at = slice(k * BLK + e, k * BLK + e + 128)
            if k < nblk_o:
                brow[:, at] = select(oid_t, (k, e), each, orows, 1, (kl, 128))
            else:
                brow[:, at] = select(mid_t, (k - nblk_o, e), each, mrows, 1, (kl, 128))
    scale = w_ref[:, pl.ds(pl.multiple_of(r * cq, 128), cq)] * (1.0 / nb_all)

    z_axis, row_axis = (Z, zi, z_dev), (R, r, row_dev)
    streams, at = [], 0
    for blocks, direct in plan(nblk):
        kind, n = (Direct, 7) if direct else (Staged, 11)
        streams.append(kind(rest[at:at + n], blocks, core, pair_dev, (z_axis, row_axis)))
        at += n

    def arrive(k):
        rows = slice(k * BLK, (k + 1) * BLK)
        arrived(x.at[rows, :], x_r.at[k])
        v = x[rows, :].astype(F32) * scale
        h = v.astype(BF16)
        xw[k, :BLK, :] = h
        xw[k, BLK:, :] = (v - h.astype(F32)).astype(BF16)

    def begin(stream):
        for k in stream.blocks:
            arrive(k)
            if len(stream.blocks) == 1 and (k + 1) * BLK == 2 * stream.H and stream.H % BLK == 0:
                stream.strip_half(k, x, xw, 1 - core)
                stream.at = 2 * stream.H
                stream.pair_start()
                stream.strip_half(k, x, xw, core)
                return
            stream.strip(k, x, xw)
        stream.pair_start()

    s1, s2, s3, s4 = streams
    begin(s1)
    s1.one_start()
    owner = lax.div(b * kc, kl)
    start = pl.multiple_of(lax.rem(b * kc, kl), 128)
    mid_c = ids[0, owner, :, pl.ds(start, kc)]
    oid_c = ids[1, owner, :, pl.ds(start, kc)]
    c_col = factors(ids[2, owner, :, pl.ds(start, kc)], tt, entries)
    bcol = [select(oid_c, (k, 0), each, orows, 0, (BLK, kc)) for k in range(nblk_o)]
    bcol += [select(mid_c, (k, 0), each, mrows, 0, (BLK, kc)) for k in range(nblk_m)]

    begin(s2)
    s2.one_start()
    s1.two_start()
    begin(s3)
    s3.one_start()
    begin(s4)
    s2.two_start()
    s4.one_start()

    t_o[...] = jnp.zeros_like(t_o)
    t_m[...] = jnp.zeros_like(t_m)
    cut = nblk_o * BLK

    def times(v, cols_of):
        a, b = split(v)
        return dot(jnp.concatenate([a, b], axis=1), jnp.concatenate([cols_of, cols_of], axis=0))

    def gather(stream):
        at = 0
        both = stream.whole()
        for k in stream.blocks:
            m = (k + 1) * BLK
            strip = both[at:at + m, :]
            at += m
            t = t_o if k < nblk_o else t_m
            t[:m, :] = t[:m, :] + times(strip, bcol[k])
            rows = slice(k * BLK, m)
            above = min(k * BLK, cut)
            if above > 0:
                part = jnp.concatenate(bcol[:above // BLK], axis=0)
                t_o[rows, :] = t_o[rows, :] + times(strip[:above, :].T, part)
            if k * BLK > cut:
                part = jnp.concatenate(bcol[nblk_o:k], axis=0)
                t_m[rows, :] = t_m[rows, :] + times(strip[cut:k * BLK, :].T, part)

    s1.back_start()
    s2.back_start()
    s3.back_start()
    s4.back_start()
    s1.spread_rest()
    s2.spread_rest()
    arrived(x.at[:n_sent, :], x_s)
    arrived(ids.at[:, :R - 1], i_s)
    for stream in streams:
        stream.settle()
    s3.pair_back()
    s1.pair_back()
    s2.pair_back()
    gather(s3)
    s4.pair_back()
    gather(s1)
    gather(s2)
    for stream in streams[:-1]:
        stream.finish()
    gather(s4)
    t = t_m[...] + t_o[...] * c_col
    t_hi, t_lo = split(t)
    step = kl // 4
    for at in range(0, kl, step):
        rows = slice(at, at + step)
        g_o = dot(brow[rows, :cut], t_hi[:cut, :]) + dot(brow[rows, :cut], t_lo[:cut, :])
        g_m = dot(brow[rows, cut:], t_hi[cut:, :]) + dot(brow[rows, cut:], t_lo[cut:, :])
        gram[rows, :] = g_m + g_o * jnp.concatenate([c_row[rows, :]] * (kc // 128), axis=1)
        pltpu.make_async_copy(gram.at[rows, :], gram_ref.at[rows, :], g_s).start()
    arrived(gram, g_s)
    s4.finish()


def plan(nblk):
    cuts = [0, nblk // 2, nblk - 2, nblk - 1, nblk]
    return [(range(a, b), i > 1) for i, (a, b) in enumerate(zip(cuts, cuts[1:]))]


def solution(mesh):
    R, B = mesh.shape["row"], mesh.shape["bus"]
    Z = B // 2

    def stream_scratch(blocks, n1, n2):
        unit = 8 * R * B
        packed = -(-(blocks * BLK) // unit) * unit
        H = packed // 2
        h1 = H // n1
        pz = h1 // n2
        dma = pltpu.SemaphoreType.DMA
        return [
            pltpu.VMEM((packed, BLK), F32),
            pltpu.VMEM((H, BLK), F32),
            pltpu.VMEM((H, BLK), F32),
            pltpu.VMEM((n1, h1, BLK), I16),
            pltpu.VMEM((n1 - 1, h1, BLK), I16),
            pltpu.VMEM((h1, BLK), F32),
            pltpu.VMEM((n2, pz, BLK), I16),
            pltpu.VMEM((n2 - 1, pz, BLK), I16),
            pltpu.VMEM((2, n1 * n2, pz, BLK), I16),
            dma((STAGED,)), dma((Z - 1,)),
        ]

    def direct_scratch(blocks):
        unit = 8 * R * B
        packed = -(-(blocks * BLK) // unit) * unit
        H = packed // 2
        n = R * Z
        dma = pltpu.SemaphoreType.DMA
        return [
            pltpu.VMEM((packed, BLK), F32),
            pltpu.VMEM((H, BLK), F32),
            pltpu.VMEM((H, BLK), F32),
            pltpu.VMEM((n, H // n, BLK), I16),
            pltpu.VMEM((n - 1, H // n, BLK), I16),
            pltpu.VMEM((2, n, H // n, BLK), I16),
            dma((DIRECT,)),
        ]

    def local(monitored, outaged, bus_weight, lodf_table, mon_id, out_id, lodf_idx):
        mrows, cols = monitored.shape
        orows = outaged.shape[0]
        n = (mrows + orows) * R
        cq = cols // R
        nblk = n // BLK
        kl = mon_id.shape[0]
        kc = kl * R // B
        hbm = pl.BlockSpec(memory_space=pl.ANY)
        dma = pltpu.SemaphoreType.DMA
        streams = plan(nblk)
        return pl.pallas_call(
            functools.partial(kernel, (R, B, cols * B)),
            out_shape=jax.ShapeDtypeStruct((kl, kc), F32),
            in_specs=[hbm] * 7,
            out_specs=hbm,
            scratch_shapes=[
                pltpu.VMEM((1, cols), F32),
                pltpu.VMEM((1, lodf_table.shape[0]), F32),
                dma((2,)),
                pltpu.VMEM((n, cq), BF16),
                pltpu.VMEM((nblk, 2 * BLK, cq), BF16),
                pltpu.VMEM((lodf_table.shape[0], 128), F32),
                pltpu.VMEM((3, R, 1, kl), jnp.int32),
                pltpu.VMEM((kl, n), BF16),
                pltpu.VMEM((n, kc), F32),
                pltpu.VMEM((n, kc), F32),
                dma, dma((nblk,)), dma, dma, pltpu.VMEM((kl, kc), F32), dma,
            ] + [
                ref for blocks, direct in streams
                for ref in (direct_scratch(sum(k + 1 for k in blocks)) if direct else
                            stream_scratch(sum(k + 1 for k in blocks), Z, R))
            ],
            compiler_params=pltpu.CompilerParams(
                collective_id=0, has_side_effects=True, vmem_limit_bytes=60 * 1024 * 1024),
        )(monitored, outaged, bus_weight[None, :], lodf_table[None, :],
          mon_id[None, :], out_id[None, :], lodf_idx[None, :])

    in_specs = (P("row", "bus"), P("row", "bus"), P("bus"), P(), P("row"), P("row"), P("row"))
    return jax.shard_map(local, mesh=mesh, in_specs=in_specs, out_specs=P("row", "bus"), check_vma=False)
```
